128 devices in a mesh: row: 8 (over y, x_lo), col: 16 (over z, x_hi, core).
Axes of the slice: x: 4 (x_hi: 2, x_lo: 2; x = x_hi * 2 + x_lo), y: 4, z: 4, core: 2. Of those that a mesh axis runs over, the one named last changes fastest.
Arguments:
- node_feats: bfloat16 [131072, 1024], P(('row', 'col')), may hold values from -6 to 6
- hub_feats: bfloat16 [4096, 1024], P('col'), may hold values from -6 to 6
- self_weight: bfloat16 [1024, 1024], replicated, may hold values from -0.1875 to 0.1875
- neigh_weight: bfloat16 [1024, 1024], replicated, may hold values from -0.1875 to 0.1875
- out_bias: float32 [1024], replicated, may hold values from -3 to 3
- tile_weights: bfloat16 [16384, 128, 128], P(('row', 'col')), may hold values from 0 to 1
- tile_blocks: int32 [128, 128], P(('row', 'col')), may hold values from 0 to 7, as said below
- send_rows: int32 [64, 2048], P('row', 'col'), may hold values from 0 to 1023
- send_count: int32 [64, 16], P('row', 'col'), may hold values from 1 to 128, as said below
- send_weight: bfloat16 [64, 2048], P('row', 'col'), may hold values from 4 to 32
- arrive_node: int32 [64, 2048], P('row', 'col'), may hold values from 0 to 1023
Outputs:
- embeddings: bfloat16 [131072, 1024], P(('row', 'col'))
The draws below stay inside these ranges and needn't reach their ends.
Inputs may be any that keep to these rules, and one draw needn't show every extreme that they name: `tile_blocks`: within one device's row of tiles, the 4 tiles of one column shard and half name distinct tile rows. `send_count`: in every column each owner sends the full 128 slots to one destination, and one destination of each column receives 128 slots from every owner.
All inputs are finite; a program needn't handle non-finite values.
Results may differ from the reference program's by a relative error of at most 0.0065.
Values may be sent and summed in bfloat16 or wider, within the bound.
No kernel may reach another device: no remote copies, remote signals or barrier semaphores. Data moves between devices by JAX's collectives and lax.ppermute only.
A program may use at most 128 MiB of HBM per device.

```python
import math
import jax
import jax.numpy as jnp
from jax import lax

D = 1024
TB = 128
NODE_DEV = 1024
NB = 8
TPH = 4
HUBS = 4096
TILES = 128
CAP = 128
NODES = 131072
N_ROW = 8
N_COL = 16


def draw_tile_blocks(key, part):
    groups = N_ROW * N_COL * N_COL * 2
    keys = jax.random.split(jax.random.fold_in(key, 11), groups)
    orders = jax.vmap(lambda one_key: jax.random.permutation(one_key, NB))(keys)
    chosen = orders[:, :TPH]
    return chosen.reshape(N_ROW * N_COL, N_COL * 2 * TPH).astype(jnp.int32)


def draw_send_count(key, part):
    key_base, key_owner, key_dest = jax.random.split(jax.random.fold_in(key, 23), 3)
    low_count = max(1, CAP // 4)
    high_count = max(low_count + 1, 3 * CAP // 4 + 1)
    base = jax.random.randint(key_base, (N_ROW, N_ROW, N_COL), low_count, high_count)
    owner_pick = jax.random.randint(key_owner, (N_ROW, N_COL), 0, N_ROW)
    owner_full = jnp.arange(N_ROW)[None, :, None] == owner_pick[:, None, :]
    dest_pick = jax.random.randint(key_dest, (N_COL,), 0, N_ROW)
    dest_full = jnp.arange(N_ROW)[None, :, None] == dest_pick[None, None, :]
    counts = jnp.where(owner_full | dest_full, CAP, base)
    return counts.reshape(N_ROW * N_ROW, N_COL).astype(jnp.int32)


def touch_ends(values, rng, low, top_value):
    spot = [jax.random.randint(jax.random.fold_in(rng, axis), (), 0, length) for axis, length in enumerate(values.shape)]
    widest = values.shape.index(max(values.shape))
    next_to = spot[:widest] + [(spot[widest] + 1) % values.shape[widest]] + spot[widest + 1:]
    return values.at[tuple(spot)].set(low).at[tuple(next_to)].set(top_value)


def block_levels(own_key, shape, pieces, smallest, top_value):
    gain, own = 1.0, jax.random.fold_in(own_key, 6)
    for dim, blocks in pieces:
        steps = jnp.exp(jax.random.uniform(jax.random.fold_in(own, dim), (blocks,), jnp.float32, smallest / len(pieces), top_value / len(pieces)))
        gain = gain * jnp.repeat(steps, shape[dim] // blocks).reshape([-1 if axis == dim else 1 for axis in range(len(shape))])
    return gain


def scatter_about(key, shape, scale, bound, cuts=(), held_as=jnp.bfloat16):
    entries = jax.random.normal(key, shape, jnp.float32) * scale
    if len(cuts) > 0:
        entries = block_levels(key, shape, cuts, -0.22, 0.18) * entries
    return jnp.clip(entries, min=-bound, max=bound).astype(held_as)


def setup_inputs(seed: int = 0) -> dict:
    key_list = jax.random.split(jax.random.key(seed), 12)
    node_feats = scatter_about(key_list[0], (NODES, D), 1.0, 6.0, ((0, 128),))
    hub_feats = scatter_about(key_list[1], (HUBS, D), 1.0, 6.0, ((0, 16),))
    self_weight = scatter_about(key_list[2], (D, D), D ** -0.5, 0.1875)
    neigh_weight = scatter_about(key_list[3], (D, D), D ** -0.5, 0.1875)
    out_bias = scatter_about(key_list[4], (D,), 0.5, 3.0, (), jnp.float32)
    tile_weights = jnp.clip(1.0 * jax.random.uniform(key_list[5], (N_ROW * N_COL * TILES, TB, TB), jnp.float32) ** block_levels(key_list[5], (N_ROW * N_COL * TILES, TB, TB), ((0, 128),), -0.2, 0.2), 0.0, 1.0).astype(jnp.bfloat16)
    tile_blocks = draw_tile_blocks(jax.random.fold_in(key_list[11], 71), 0)
    send_rows = touch_ends(jax.random.randint(key_list[7], (N_ROW * N_ROW, N_COL * CAP), 0, NODE_DEV), jax.random.fold_in(key_list[7], 1), 0, NODE_DEV - 1).astype(jnp.int32)
    send_count = draw_send_count(jax.random.fold_in(key_list[11], 71), 0)
    send_weight = jnp.clip(jnp.exp(math.log(32.0) - 2.0794415 * jax.random.uniform(key_list[9], (N_ROW * N_ROW, N_COL * CAP), jnp.float32) ** block_levels(key_list[9], (N_ROW * N_ROW, N_COL * CAP), ((0, 8), (1, 16)), -0.2, 0.2)), 4.0, 32.0).astype(jnp.bfloat16)
    arrive_node = touch_ends(jax.random.randint(key_list[10], (N_ROW * N_ROW, N_COL * CAP), 0, NODE_DEV), jax.random.fold_in(key_list[10], 1), 0, NODE_DEV - 1).astype(jnp.int32)
    return {"node_feats": node_feats, "hub_feats": hub_feats, "self_weight": self_weight, "neigh_weight": neigh_weight, "out_bias": out_bias, "tile_weights": tile_weights, "tile_blocks": tile_blocks, "send_rows": send_rows, "send_count": send_count, "send_weight": send_weight, "arrive_node": arrive_node}


def reference(node_feats, hub_feats, self_weight, neigh_weight, out_bias, tile_weights, tile_blocks, send_rows, send_count, send_weight, arrive_node):
    node_table = node_feats.reshape(N_ROW, N_COL, NODE_DEV, D)
    hub_halves = hub_feats.reshape(N_COL, 2, TB, D).astype(jnp.float32)
    tile_table = tile_weights.reshape(N_ROW * N_COL, N_COL, 2, TPH, TB, TB)
    block_table = tile_blocks.reshape(N_ROW * N_COL, N_COL * 2 * TPH)
    send_table = send_rows.reshape(N_ROW, N_ROW, N_COL, CAP)
    weight_table = send_weight.reshape(N_ROW, N_ROW, N_COL, CAP)
    count_table = send_count.reshape(N_ROW, N_ROW, N_COL)
    arrive_table = arrive_node.reshape(N_ROW, N_ROW, N_COL, CAP)

    def one_device(device):
        row_index = device // N_COL
        col_index = device % N_COL
        own_tiles = tile_table[device].astype(jnp.float32)
        products = jnp.einsum('shtij,shjd->shtid', own_tiles, hub_halves).reshape(-1, TB, D)
        own_blocks = block_table[device]
        hub_sum = jnp.zeros((NB, TB, D), jnp.float32).at[own_blocks].add(products)
        row_sums = lax.optimization_barrier(jnp.sum(own_tiles, axis=-1)).reshape(-1, TB)
        hub_weight = jnp.zeros((NB, TB), jnp.float32).at[own_blocks].add(row_sums)
        owner_feats = node_table[:, col_index]
        slot_rows = send_table[:, row_index, col_index]
        picked = jax.vmap(lambda feats, rows: feats[rows])(owner_feats, slot_rows)
        tail_weights = weight_table[:, row_index, col_index].astype(jnp.float32)
        counts = count_table[:, row_index, col_index]
        usable = jnp.arange(CAP, dtype=jnp.int32)[None, :] < counts[:, None]
        message = jnp.where(usable[:, :, None], tail_weights[:, :, None] * picked.astype(jnp.float32), 0.0).astype(jnp.bfloat16)
        kept_weight = jnp.where(usable, tail_weights, 0.0)
        arrive_at = arrive_table[row_index, :, col_index].reshape(-1)
        tail_sum = jax.ops.segment_sum(message.astype(jnp.float32).reshape(-1, D), arrive_at, num_segments=NODE_DEV)
        tail_weight = jax.ops.segment_sum(kept_weight.reshape(-1), arrive_at, num_segments=NODE_DEV)
        combined = hub_sum.reshape(NODE_DEV, D) + tail_sum
        weight_sum = hub_weight.reshape(NODE_DEV) + tail_weight
        neighbour = (combined * lax.rsqrt(1.0 + weight_sum)[:, None]).astype(jnp.bfloat16)
        own_feats = node_table[row_index, col_index]
        preact = jnp.dot(own_feats, self_weight, preferred_element_type=jnp.float32)
        preact = preact + jnp.dot(neighbour, neigh_weight, preferred_element_type=jnp.float32) + out_bias
        hidden = jnp.maximum(preact, 0.0)
        row_scale = lax.rsqrt(lax.optimization_barrier(jnp.mean(hidden * hidden, axis=-1, keepdims=True)) + 1e-06)
        return (hidden * row_scale).astype(jnp.bfloat16)
    results = lax.map(one_device, jnp.arange(N_ROW * N_COL, dtype=jnp.int32))
    return results.reshape(N_ROW * N_COL * NODE_DEV, D)
```

```python
import numpy as np
import jax
import jax.numpy as jnp
from jax import lax
from jax.experimental import pallas as pl
from jax.experimental.pallas import tpu as pltpu
from jax.sharding import PartitionSpec as P

MESH_AXES = ("row", "col")
D = 1024
TB = 128
NODES = 1024
SLOTS = 128
PAD = 8
MIB = 1 << 20


def flat(y, xl, z, xh, k):
    return (y * 2 + xl) * 16 + z * 4 + xh * 2 + k


def pairs_of(move):
    pairs = []
    for source in range(128):
        row, col = divmod(source, 16)
        place = (row // 2, row % 2, col // 4, (col // 2) % 2, col % 2)
        pairs.append((source, flat(*move(*place))))
    return pairs


ACROSS = pairs_of(lambda y, xl, z, xh, k: (y, 1 - xl, z, 1 - xh, k))
UP = pairs_of(lambda y, xl, z, xh, k: (y, xl, (z + 1) % 4, xh, k))
DOWN = pairs_of(lambda y, xl, z, xh, k: (y, xl, (z - 1) % 4, xh, k))
CORE = pairs_of(lambda y, xl, z, xh, k: (y, xl, z, xh, 1 - k))


def send(value, pairs):
    return lax.ppermute(value, MESH_AXES, pairs)


def both_cores(halves):
    return [(dz, dx, 0, h) for dz, dx, h in halves] + [(dz, dx, 1, h) for dz, dx, h in halves]


def whole(dz, dx):
    return [(dz, dx, 0), (dz, dx, 1)]


FIRST = [(0, 0, 0, 0), (0, 0, 0, 1), (0, 0, 1, 0), (0, 0, 1, 1)] + both_cores(
    whole(0, 1) + whole(-1, 0) + whole(1, 0)
)
SECOND = both_cores([(-1, 1, 0), (2, 0, 0), (-1, 1, 1), (1, 1, 0), (1, 1, 1), (2, 0, 1)])
THIRD = both_cores([(2, 1, 0), (2, 1, 1)])
ORDER = np.array(FIRST + SECOND + THIRD, np.int32)


def half_order():
    col = lax.axis_index("col").astype(jnp.int32)
    z, xh, k = col // 4, (col // 2) % 2, col % 2
    dz, dx, dk, h = (jnp.asarray(ORDER[:, i]) for i in range(4))
    shard = ((z + dz) % 4) * 4 + (xh ^ dx) * 2 + (k ^ dk)
    return shard * 2 + h


def message_kernel(count_ref, rows_ref, weight_ref, feats_ref, out_ref, hot_ref):
    slot = lax.broadcasted_iota(jnp.int32, (1, SLOTS), 1)
    kept = [
        jnp.where(slot < count_ref[d], weight_ref[d : d + 1, :].astype(jnp.float32), 0.0)
        for d in range(8)
    ]
    kept = jnp.concatenate(kept, axis=0)
    kept_t = jnp.transpose(kept)

    @pl.when(pl.program_id(0) == 0)
    def _():
        rows_t = jnp.transpose(rows_ref[...])
        node = lax.broadcasted_iota(jnp.int32, (SLOTS, NODES), 1)
        for d in range(8):
            hot_ref[d * SLOTS : (d + 1) * SLOTS, :] = jnp.where(
                rows_t[:, d : d + 1] == node, 1.0, 0.0
            ).astype(jnp.bfloat16)

    picked = jnp.dot(hot_ref[...], feats_ref[...], preferred_element_type=jnp.float32)
    for d in range(8):
        block = picked[d * SLOTS : (d + 1) * SLOTS, :] * kept_t[:, d : d + 1]
        out_ref[d, 0:SLOTS, :] = block.astype(jnp.bfloat16)
        line = jnp.broadcast_to(kept[d : d + 1, :], (PAD, SLOTS)).astype(jnp.bfloat16)
        out_ref[d, SLOTS : SLOTS + PAD, 0:SLOTS] = line
        out_ref[d, SLOTS : SLOTS + PAD, SLOTS:] = jnp.zeros_like(
            out_ref[d, SLOTS : SLOTS + PAD, SLOTS:]
        )


def messages(node_feats, send_rows, send_count, send_weight):
    tn = 256
    return pl.pallas_call(
        message_kernel,
        grid_spec=pltpu.PrefetchScalarGridSpec(
            num_scalar_prefetch=1,
            grid=(D // tn,),
            in_specs=[
                pl.BlockSpec((8, SLOTS), lambda j, c: (0, 0)),
                pl.BlockSpec((8, SLOTS), lambda j, c: (0, 0)),
                pl.BlockSpec((NODES, tn), lambda j, c: (0, j)),
            ],
            out_specs=pl.BlockSpec((8, SLOTS + PAD, tn), lambda j, c: (0, 0, j)),
            scratch_shapes=[pltpu.VMEM((NODES, NODES), jnp.bfloat16)],
        ),
        out_shape=jax.ShapeDtypeStruct((8, SLOTS + PAD, D), jnp.bfloat16),
        compiler_params=pltpu.CompilerParams(vmem_limit_bytes=16 * MIB),
        name="messages",
    )(send_count.reshape(8), send_rows, send_weight, node_feats)


PER_STEP = 4


def place_kernel(order_ref, blocks_ref, *refs):
    tiles = refs[:PER_STEP]
    out_ref, sums_ref = refs[PER_STEP:]
    step = pl.program_id(0)

    @pl.when(step == 0)
    def _():
        sums_ref[...] = jnp.zeros_like(sums_ref)

    out_ref[...] = jnp.zeros_like(out_ref)
    for q in range(PER_STEP):
        first = order_ref[step * PER_STEP + q] * 4
        for t in range(4):
            at = pl.multiple_of(blocks_ref[first + t] * TB, TB)
            tile = tiles[q][t]
            out_ref[pl.ds(at, TB), q * TB : (q + 1) * TB] = tile
            sums_ref[pl.ds(at, TB), :] += tile.astype(jnp.float32)


def placed_tiles(order, tile_blocks, tile_weights):
    def tile_spec(q):
        return pl.BlockSpec((4, TB, TB), lambda i, o, b: (o[i * PER_STEP + q], 0, 0))

    return pl.pallas_call(
        place_kernel,
        grid_spec=pltpu.PrefetchScalarGridSpec(
            num_scalar_prefetch=2,
            grid=(32 // PER_STEP,),
            in_specs=[tile_spec(q) for q in range(PER_STEP)],
            out_specs=[
                pl.BlockSpec((NODES, PER_STEP * TB), lambda i, o, b: (0, i)),
                pl.BlockSpec((NODES, TB), lambda i, o, b: (0, 0)),
            ],
        ),
        out_shape=[
            jax.ShapeDtypeStruct((NODES, 32 * TB), jnp.bfloat16),
            jax.ShapeDtypeStruct((NODES, TB), jnp.float32),
        ],
        compiler_params=pltpu.CompilerParams(vmem_limit_bytes=16 * MIB),
        name="placed_tiles",
    )(order, tile_blocks.reshape(128), *([tile_weights] * PER_STEP))


def self_kernel(feats_ref, weight_ref, bias_ref, out_ref):
    out_ref[...] = (
        jnp.dot(feats_ref[...], weight_ref[...], preferred_element_type=jnp.float32)
        + bias_ref[...]
    )


def self_part(node_feats, self_weight, out_bias):
    tm = 256
    return pl.pallas_call(
        self_kernel,
        grid=(NODES // tm,),
        in_specs=[
            pl.BlockSpec((tm, D), lambda i: (i, 0)),
            pl.BlockSpec((D, D), lambda i: (0, 0)),
            pl.BlockSpec((1, D), lambda i: (0, 0)),
        ],
        out_specs=pl.BlockSpec((tm, D), lambda i: (i, 0)),
        out_shape=jax.ShapeDtypeStruct((NODES, D), jnp.float32),
        compiler_params=pltpu.CompilerParams(vmem_limit_bytes=16 * MIB),
        name="self_part",
    )(node_feats, self_weight, out_bias.reshape(1, D))


def stack(parts, hub_ref):
    at = 0
    for part in parts:
        rows = part.shape[0]
        hub_ref[at : at + rows, :] = part[...]
        at += rows


def hub_kernel(placed_ref, *refs, count, carried):
    parts = refs[:count]
    refs = refs[count:]
    out_ref, hub_ref = refs[-2:]

    @pl.when(pl.program_id(0) == 0)
    def _():
        stack(parts, hub_ref)

    product = jnp.dot(placed_ref[...], hub_ref[...], preferred_element_type=jnp.float32)
    if carried:
        product = product + refs[0][...]
    out_ref[...] = product


def hub_products(placed, first, parts, carry=None):
    tm = 256
    width = sum(part.shape[0] for part in parts)
    column = first // width if first % width == 0 else None
    operands = [placed, *parts]
    if column is None:
        spec = pl.BlockSpec((pl.Element(tm), pl.Element(width)), lambda i: (i * tm, first))
    else:
        spec = pl.BlockSpec((tm, width), lambda i: (i, column))
    in_specs = [spec]
    in_specs += [pl.BlockSpec(part.shape, lambda i: (0, 0)) for part in parts]
    if carry is not None:
        in_specs.append(pl.BlockSpec((tm, D), lambda i: (i, 0)))
        operands.append(carry)

    def body(*refs):
        hub_kernel(*refs, count=len(parts), carried=carry is not None)

    return pl.pallas_call(
        body,
        grid=(NODES // tm,),
        in_specs=in_specs,
        out_specs=pl.BlockSpec((tm, D), lambda i: (i, 0)),
        out_shape=jax.ShapeDtypeStruct((NODES, D), jnp.float32),
        scratch_shapes=[pltpu.VMEM((width, D), jnp.bfloat16)],
        compiler_params=pltpu.CompilerParams(vmem_limit_bytes=32 * MIB),
        name="hub_products",
    )(*operands)


def last_kernel(
    placed_ref, f0, f1, c0, c1, sums_ref, carry_ref, base_ref, at_ref, got_ref, line_ref,
    weight_ref, out_ref, hub_ref, hot_ref,
):
    tm = out_ref.shape[0]
    step = pl.program_id(0)

    @pl.when(step == 0)
    def _():
        stack((f0, f1, c0, c1), hub_ref)

    node = lax.broadcasted_iota(jnp.int32, (tm, SLOTS), 0) + step * tm
    weights = sums_ref[...]
    for o in range(8):
        hit = at_ref[o : o + 1, :] == node
        hot_ref[:, o * SLOTS : (o + 1) * SLOTS] = jnp.where(hit, 1.0, 0.0).astype(jnp.bfloat16)
        line = line_ref[o, 0:1, 0:SLOTS].astype(jnp.float32)
        weights = weights + jnp.where(hit, line, 0.0)
    weight_sum = jnp.sum(weights, axis=-1, keepdims=True)
    combined = carry_ref[...] + jnp.dot(
        placed_ref[...], hub_ref[...], preferred_element_type=jnp.float32
    )
    combined = combined + jnp.dot(
        hot_ref[...],
        got_ref[...].reshape(8 * SLOTS, D),
        preferred_element_type=jnp.float32,
    )
    neighbour = (combined * lax.rsqrt(1.0 + weight_sum)).astype(jnp.bfloat16)
    preact = base_ref[...] + jnp.dot(
        neighbour, weight_ref[...], preferred_element_type=jnp.float32
    )
    hidden = jnp.maximum(preact, 0.0)
    scale = lax.rsqrt(jnp.mean(hidden * hidden, axis=-1, keepdims=True) + 1e-06)
    out_ref[...] = (hidden * scale).astype(jnp.bfloat16)


def last_part(placed, parts, sums, carry, base, arrive_node, arrived, neigh_weight):
    tm = 256
    width = 512
    column = placed.shape[1] // width - 1
    return pl.pallas_call(
        last_kernel,
        grid=(NODES // tm,),
        in_specs=[pl.BlockSpec((tm, width), lambda i: (i, column))]
        + [pl.BlockSpec(part.shape, lambda i: (0, 0)) for part in parts]
        + [
            pl.BlockSpec((tm, TB), lambda i: (i, 0)),
            pl.BlockSpec((tm, D), lambda i: (i, 0)),
            pl.BlockSpec((tm, D), lambda i: (i, 0)),
            pl.BlockSpec((8, SLOTS), lambda i: (0, 0)),
            pl.BlockSpec((8, SLOTS, D), lambda i: (0, 0, 0)),
            pl.BlockSpec((8, PAD, SLOTS), lambda i: (0, SLOTS // PAD, 0)),
            pl.BlockSpec((D, D), lambda i: (0, 0)),
        ],
        out_specs=pl.BlockSpec((tm, D), lambda i: (i, 0)),
        out_shape=jax.ShapeDtypeStruct((NODES, D), jnp.bfloat16),
        scratch_shapes=[
            pltpu.VMEM((width, D), jnp.bfloat16),
            pltpu.VMEM((tm, 8 * SLOTS), jnp.bfloat16),
        ],
        compiler_params=pltpu.CompilerParams(vmem_limit_bytes=32 * MIB),
        name="last_part",
    )(placed, *parts, sums, carry, base, arrive_node, arrived, arrived, neigh_weight)


def shards(
    node_feats,
    hub_feats,
    self_weight,
    neigh_weight,
    out_bias,
    tile_weights,
    tile_blocks,
    send_rows,
    send_count,
    send_weight,
    arrive_node,
):
    own = hub_feats
    across = send(own, ACROSS)
    up = send(own, UP)
    down = send(own, DOWN)
    own_c = send(own, CORE)

    message = messages(node_feats, send_rows, send_count, send_weight)
    arrived = lax.all_to_all(message, "row", split_axis=0, concat_axis=0, tiled=True)

    placed, sums = placed_tiles(half_order(), tile_blocks, tile_weights)
    base = self_part(node_feats, self_weight, out_bias)

    up2 = send(jnp.concatenate([across[:TB], up[:TB]], 0), UP)
    down2 = send(jnp.concatenate([across[TB:], down[TB:]], 0), DOWN)
    across2 = send(jnp.concatenate([up[TB:], down[:TB]], 0), ACROSS)
    across_c = send(across, CORE)
    up_c = send(up, CORE)
    down_c = send(down, CORE)

    carry = hub_products(
        placed, 0, [own, own_c, across, up, down, across_c, up_c, down_c]
    )

    up3 = send(up2[:TB], UP)
    down3 = send(down2[:TB], DOWN)
    up2_c = send(up2, CORE)
    across2_c = send(across2, CORE)
    down2_c = send(down2, CORE)
    carry = hub_products(
        placed, 2048, [up2, across2, down2, up2_c, across2_c, down2_c], carry
    )
    up3_c = send(up3, CORE)
    down3_c = send(down3, CORE)
    return last_part(
        placed,
        [up3, down3, up3_c, down3_c],
        sums,
        carry,
        base,
        arrive_node,
        arrived,
        neigh_weight,
    )


def solution(mesh):
    placed = (
        P(("row", "col"), None),
        P("col", None),
        P(),
        P(),
        P(),
        P(("row", "col"), None, None),
        P(("row", "col"), None),
        P("row", "col"),
        P("row", "col"),
        P("row", "col"),
        P("row", "col"),
    )
    return jax.shard_map(
        shards, mesh=mesh, in_specs=placed, out_specs=P(("row", "col"), None), check_vma=False
    )
```

```python
import numpy as np
import jax
import jax.numpy as jnp
from jax import lax
from jax.experimental import pallas as pl
from jax.experimental.pallas import tpu as pltpu
from jax.sharding import PartitionSpec as P

MESH_AXES = ("row", "col")
D = 1024
TB = 128
NODES = 1024
SLOTS = 128
PAD = 8
MIB = 1 << 20


def flat(y, xl, z, xh, k):
    return (y * 2 + xl) * 16 + z * 4 + xh * 2 + k


def pairs_of(move):
    pairs = []
    for source in range(128):
        row, col = divmod(source, 16)
        place = (row // 2, row % 2, col // 4, (col // 2) % 2, col % 2)
        pairs.append((source, flat(*move(*place))))
    return pairs


ACROSS = pairs_of(lambda y, xl, z, xh, k: (y, 1 - xl, z, 1 - xh, k))
UP = pairs_of(lambda y, xl, z, xh, k: (y, xl, (z + 1) % 4, xh, k))
DOWN = pairs_of(lambda y, xl, z, xh, k: (y, xl, (z - 1) % 4, xh, k))
CORE = pairs_of(lambda y, xl, z, xh, k: (y, xl, z, xh, 1 - k))


def send(value, pairs):
    return lax.ppermute(value, MESH_AXES, pairs)


def both_cores(*steps):
    return [(dz, dx, k, h) for k in (0, 1) for dz, dx in steps for h in (0, 1)]


FIRST = both_cores((0, 0), (0, 1), (-1, 0), (1, 0))
LATER = ((-1, 1), (1, 1), (2, 1))
SECOND = both_cores((2, 0)) + both_cores(*LATER)[: 2 * len(LATER)]
THIRD = both_cores(*LATER)[2 * len(LATER) :]
ORDER = np.array(FIRST + SECOND + THIRD, np.int32)


def half_order():
    col = lax.axis_index("col").astype(jnp.int32)
    z, xh, k = col // 4, (col // 2) % 2, col % 2
    dz, dx, dk, h = (jnp.asarray(ORDER[:, i]) for i in range(4))
    shard = ((z + dz) % 4) * 4 + (xh ^ dx) * 2 + (k ^ dk)
    return shard * 2 + h


ROWS = pl.BlockSpec(memory_space=pltpu.VMEM)
FAR = pl.BlockSpec(memory_space=pltpu.HBM)
WORDS = pl.BlockSpec(memory_space=pltpu.SMEM)


def near(value):
    return pltpu.with_memory_space_constraint(value, pltpu.VMEM)


def far(value):
    return pltpu.with_memory_space_constraint(value, pltpu.HBM)


def params(mib):
    return pltpu.CompilerParams(vmem_limit_bytes=mib * MIB)


SHARE = 4


def cost(flops, nbytes):
    return pl.CostEstimate(flops=flops // SHARE, transcendentals=0, bytes_accessed=nbytes // SHARE)


def product(left, right):
    return jnp.dot(left, right, preferred_element_type=jnp.float32)


def message_kernel(count_ref, rows_ref, weight_ref, feats_ref, out_ref, stage_ref, sems):
    slot = lax.broadcasted_iota(jnp.int32, (1, SLOTS), 1)
    kept = [
        jnp.where(slot < count_ref[d], weight_ref[d : d + 1, :].astype(jnp.float32), 0.0)
        for d in range(8)
    ]
    kept = jnp.concatenate(kept, axis=0)
    kept_t = jnp.transpose(kept)
    rows_t = jnp.transpose(rows_ref[...])
    node = lax.broadcasted_iota(jnp.int32, (SLOTS, NODES), 1)
    copies = []
    for pair in range(4):
        hot = [
            jnp.where(rows_t[:, d : d + 1] == node, 1.0, 0.0).astype(jnp.bfloat16)
            for d in (2 * pair, 2 * pair + 1)
        ]
        picked = product(jnp.concatenate(hot, axis=0), feats_ref[...])
        for q in range(2):
            d = 2 * pair + q
            block = picked[q * SLOTS : (q + 1) * SLOTS, :] * kept_t[:, d : d + 1]
            stage_ref[d, 0:SLOTS, :] = block.astype(jnp.bfloat16)
            line = jnp.broadcast_to(kept[d : d + 1, :], (PAD, SLOTS)).astype(jnp.bfloat16)
            stage_ref[d, SLOTS : SLOTS + PAD, 0:SLOTS] = line
            stage_ref[d, SLOTS : SLOTS + PAD, SLOTS:] = jnp.zeros(
                (PAD, D - SLOTS), jnp.bfloat16
            )
            copy = pltpu.make_async_copy(stage_ref.at[d], out_ref.at[d], sems.at[d])
            copy.start()
            copies.append(copy)
    for copy in copies:
        copy.wait()


def messages(node_feats, send_rows, send_count, send_weight):
    return pl.pallas_call(
        message_kernel,
        in_specs=[WORDS, ROWS, ROWS, ROWS],
        out_specs=FAR,
        out_shape=pltpu.HBM((8, SLOTS + PAD, D), jnp.bfloat16),
        scratch_shapes=[
            pltpu.VMEM((8, SLOTS + PAD, D), jnp.bfloat16),
            pltpu.SemaphoreType.DMA((8,)),
        ],
        compiler_params=params(8),
        cost_estimate=cost(2 * NODES * NODES * D, 5 * MIB),
        name="messages",
    )(send_count.reshape(8), near(send_rows), near(send_weight), near(node_feats))


LATE = len(THIRD)
EARLY = len(FIRST) + len(SECOND)


def place_kernel(
    order_ref, blocks_ref, tiles_ref, early_ref, late_ref, sums_ref, stage_ref, tally_ref, sems
):
    tally_ref[...] = jnp.zeros_like(tally_ref)
    stage_ref[...] = jnp.zeros_like(stage_ref)
    early_ref[...] = jnp.zeros_like(early_ref)

    def place(p, ref, column):
        first = order_ref[p] * 4
        for t in range(4):
            at = pl.multiple_of(blocks_ref[first + t] * TB, TB)
            tile = tiles_ref[first + t]
            ref[pl.ds(at, TB), column * TB : (column + 1) * TB] = tile
            tally_ref[pl.ds(at, TB), :] += tile.astype(jnp.float32)

    for p in range(LATE):
        place(EARLY + p, stage_ref, p)
    late_copy = pltpu.make_async_copy(stage_ref, late_ref, sems.at[0])
    late_copy.start()
    for p in range(EARLY):
        place(p, early_ref, p)
    sums_copy = pltpu.make_async_copy(tally_ref, sums_ref, sems.at[1])
    sums_copy.start()
    late_copy.wait()
    sums_copy.wait()


def placed_tiles(order, tile_blocks, tile_weights):
    return pl.pallas_call(
        place_kernel,
        in_specs=[WORDS, WORDS, ROWS],
        out_specs=[ROWS, FAR, FAR],
        out_shape=[
            pltpu.VMEM((NODES, EARLY * TB), jnp.bfloat16),
            pltpu.HBM((NODES, LATE * TB), jnp.bfloat16),
            pltpu.HBM((NODES, TB), jnp.float32),
        ],
        scratch_shapes=[
            pltpu.VMEM((NODES, LATE * TB), jnp.bfloat16),
            pltpu.VMEM((NODES, TB), jnp.float32),
            pltpu.SemaphoreType.DMA((2,)),
        ],
        compiler_params=params(6),
        cost_estimate=cost(0, 12 * MIB),
        name="placed_tiles",
    )(order, tile_blocks.reshape(128), near(tile_weights))


def self_kernel(feats_ref, weight_ref, bias_ref, out_ref, stage_ref, sems):
    copies = []
    for step in range(4):
        lanes = slice(step * 256, (step + 1) * 256)
        stage_ref[:, lanes] = product(feats_ref[...], weight_ref[:, lanes]) + bias_ref[:, lanes]
        copy = pltpu.make_async_copy(
            stage_ref.at[:, lanes], out_ref.at[:, lanes], sems.at[step]
        )
        copy.start()
        copies.append(copy)
    for copy in copies:
        copy.wait()


def self_part(node_feats, self_weight, out_bias):
    return pl.pallas_call(
        self_kernel,
        in_specs=[ROWS, ROWS, ROWS],
        out_specs=FAR,
        out_shape=pltpu.HBM((NODES, D), jnp.float32),
        scratch_shapes=[
            pltpu.VMEM((NODES, D), jnp.float32),
            pltpu.SemaphoreType.DMA((4,)),
        ],
        compiler_params=params(8),
        cost_estimate=cost(2 * NODES * D * D, 8 * MIB),
        name="self_part",
    )(near(node_feats), near(self_weight), near(out_bias.reshape(1, D)))


def hub_products(placed, first, parts, carry=None):
    width = sum(part.shape[0] for part in parts)
    operands = [near(placed), *[near(part) for part in parts]]
    if carry is not None:
        operands.append(near(carry))

    def body(placed_ref, *refs):
        if carry is None:
            stage_ref = refs[-1]
        else:
            out_ref, stage_ref, sems = refs[-3:]
        copies = []
        for step in range(4):
            lanes = slice(step * 256, (step + 1) * 256)
            hubs = jnp.concatenate([ref[:, lanes] for ref in refs[: len(parts)]], axis=0)
            total = product(placed_ref[:, first : first + width], hubs)
            if carry is not None:
                total = total + refs[len(parts)][:, lanes]
            stage_ref[:, lanes] = total
            if carry is not None:
                copy = pltpu.make_async_copy(
                    stage_ref.at[:, lanes], out_ref.at[:, lanes], sems.at[step]
                )
                copy.start()
                copies.append(copy)
        for copy in copies:
            copy.wait()

    stage = pltpu.VMEM((NODES, D), jnp.float32)
    return pl.pallas_call(
        body,
        in_specs=[ROWS] * len(operands),
        out_specs=ROWS if carry is None else FAR,
        out_shape=stage if carry is None else pltpu.HBM((NODES, D), jnp.float32),
        scratch_shapes=[] if carry is None else [stage, pltpu.SemaphoreType.DMA((4,))],
        compiler_params=params(8 if carry is None else 10),
        cost_estimate=cost(2 * NODES * width * D, 10 * MIB),
        name="hub_products",
    )(*operands)


def last_part(placed, parts, sums, carry, base, arrive_node, arrived, neigh_weight):
    width = sum(part.shape[0] for part in parts)
    tm = 256
    steps = NODES // tm

    def body(
        got_ref, at_ref, placed_hbm, part_a, part_b, part_c, sums_hbm, carry_hbm, base_hbm,
        weight_hbm, out_ref, placed_ref, hub_ref, sums_ref, carry_ref, base_ref, weight_ref, stage_ref,
        in_sems, out_sems,
    ):
        third = width // 3

        def rows(step):
            return slice(step * tm, (step + 1) * tm)

        loads = [
            (part_a, hub_ref.at[0:third]),
            (part_b, hub_ref.at[third : 2 * third]),
            (part_c, hub_ref.at[2 * third :]),
            (placed_hbm, placed_ref),
            (sums_hbm, sums_ref),
            (carry_hbm.at[rows(0)], carry_ref.at[rows(0)]),
            (weight_hbm, weight_ref),
            (base_hbm.at[rows(0)], base_ref.at[rows(0)]),
        ]
        for step in range(1, steps):
            loads.append((carry_hbm.at[rows(step)], carry_ref.at[rows(step)]))
            loads.append((base_hbm.at[rows(step)], base_ref.at[rows(step)]))
        loads = [
            pltpu.make_async_copy(source, target, in_sems.at[i])
            for i, (source, target) in enumerate(loads)
        ]
        for load in loads:
            load.start()
        copies = []
        for step in range(steps):
            here = rows(step)
            node = lax.broadcasted_iota(jnp.int32, (tm, SLOTS), 0) + step * tm
            weights = jnp.zeros((tm, SLOTS), jnp.float32)
            hot = []
            for o in range(8):
                hit = at_ref[o : o + 1, :] == node
                hot.append(jnp.where(hit, 1.0, 0.0).astype(jnp.bfloat16))
                line = got_ref[o, SLOTS : SLOTS + 1, 0:SLOTS].astype(jnp.float32)
                weights = weights + jnp.where(hit, line, 0.0)
            got = jnp.concatenate([got_ref[o, 0:SLOTS, :] for o in range(8)], axis=0)
            combined = product(jnp.concatenate(hot, axis=1), got)
            if step == 0:
                for load in loads[:6]:
                    load.wait()
            else:
                loads[6 + 2 * step].wait()
            weight_sum = jnp.sum(weights + sums_ref[here, :], axis=-1, keepdims=True)
            combined = combined + product(placed_ref[here, :], hub_ref[...])
            combined = combined + carry_ref[here, :]
            neighbour = (combined * lax.rsqrt(1.0 + weight_sum)).astype(jnp.bfloat16)
            if step == 0:
                loads[6].wait()
            loads[7 + 2 * step].wait()
            preact = base_ref[here, :] + product(neighbour, weight_ref[...])
            hidden = jnp.maximum(preact, 0.0)
            scale = lax.rsqrt(jnp.mean(hidden * hidden, axis=-1, keepdims=True) + 1e-06)
            stage_ref[here, :] = (hidden * scale).astype(jnp.bfloat16)
            copy = pltpu.make_async_copy(
                stage_ref.at[here], out_ref.at[here], out_sems.at[step]
            )
            copy.start()
            copies.append(copy)
        for copy in copies:
            copy.wait()

    return pl.pallas_call(
        body,
        in_specs=[ROWS, ROWS] + [FAR] * 8,
        out_specs=FAR,
        out_shape=pltpu.HBM((NODES, D), jnp.bfloat16),
        scratch_shapes=[
            pltpu.VMEM((NODES, width), jnp.bfloat16),
            pltpu.VMEM((width, D), jnp.bfloat16),
            pltpu.VMEM((NODES, TB), jnp.float32),
            pltpu.VMEM((NODES, D), jnp.float32),
            pltpu.VMEM((NODES, D), jnp.float32),
            pltpu.VMEM((D, D), jnp.bfloat16),
            pltpu.VMEM((NODES, D), jnp.bfloat16),
            pltpu.SemaphoreType.DMA((7 + 2 * steps,)),
            pltpu.SemaphoreType.DMA((steps,)),
        ],
        compiler_params=params(26),
        cost_estimate=cost(2 * NODES * D * (width + 2 * D), 16 * MIB),
        name="last_part",
    )(
        near(arrived), near(arrive_node),
        *[far(value) for value in (placed, *parts, sums, carry, base, neigh_weight)],
    )


def after(value, *others):
    return lax.optimization_barrier((value, *others))[0]


def shards(
    node_feats,
    hub_feats,
    self_weight,
    neigh_weight,
    out_bias,
    tile_weights,
    tile_blocks,
    send_rows,
    send_count,
    send_weight,
    arrive_node,
):
    own = hub_feats
    across = send(own, ACROSS)
    up = send(own, UP)
    down = send(own, DOWN)

    order, node_feats = lax.optimization_barrier((half_order(), node_feats))
    message = messages(node_feats, send_rows, send_count, send_weight)
    own_k, order, message = lax.optimization_barrier((own, order, message))
    arrived = lax.all_to_all(message, "row", split_axis=0, concat_axis=0, tiled=True)
    own_c = send(own_k, CORE)
    placed, placed_late, sums = placed_tiles(order, tile_blocks, tile_weights)

    up, down, across, own_c, placed = lax.optimization_barrier(
        (up, down, across, own_c, placed)
    )
    two_low = send(up[:TB], UP)
    two_high = send(down[TB:], DOWN)
    across_c = send(across, CORE)
    up_c = send(up, CORE)
    down_c = send(down, CORE)
    base = self_part(node_feats, self_weight, out_bias)

    two_low, two_high, across, across_c, up_c, down_c, base = lax.optimization_barrier(
        (two_low, two_high, across, across_c, up_c, down_c, base)
    )
    two = jnp.concatenate([two_low, two_high], 0)
    up_x = send(across, UP)
    down_x = send(across, DOWN)
    two_x = send(two, ACROSS)
    two_c = send(two, CORE)
    carry = hub_products(
        placed, 0, [own, across, up, down, own_c, across_c, up_c, down_c]
    )

    up_x, down_x, two_x, two_c, carry = lax.optimization_barrier(
        (up_x, down_x, two_x, two_c, carry)
    )
    late = [send(part, CORE) for part in (up_x, down_x, two_x)]
    carry = hub_products(placed, 2048, [two, two_c, up_x, down_x, two_x], carry)
    return last_part(
        placed_late, late, sums, carry, base, arrive_node, arrived, neigh_weight
    )


def solution(mesh):
    placed = (
        P(("row", "col"), None),
        P("col", None),
        P(),
        P(),
        P(),
        P(("row", "col"), None, None),
        P(("row", "col"), None),
        P("row", "col"),
        P("row", "col"),
        P("row", "col"),
        P("row", "col"),
    )
    return jax.shard_map(
        shards, mesh=mesh, in_specs=placed, out_specs=P(("row", "col"), None), check_vma=False
    )
```

```python
import numpy as np
import jax
import jax.numpy as jnp
from jax import lax
from jax.experimental import pallas as pl
from jax.experimental.pallas import tpu as pltpu
from jax.sharding import PartitionSpec as P

MESH_AXES = ("row", "col")
D = 1024
TB = 128
NODES = 1024
SLOTS = 128
PAD = 8
MIB = 1 << 20


def flat(y, xl, z, xh, k):
    return (y * 2 + xl) * 16 + z * 4 + xh * 2 + k


def pairs_of(move):
    pairs = []
    for source in range(128):
        row, col = divmod(source, 16)
        place = (row // 2, row % 2, col // 4, (col // 2) % 2, col % 2)
        pairs.append((source, flat(*move(*place))))
    return pairs


ACROSS = pairs_of(lambda y, xl, z, xh, k: (y, 1 - xl, z, 1 - xh, k))
UP = pairs_of(lambda y, xl, z, xh, k: (y, xl, (z + 1) % 4, xh, k))
DOWN = pairs_of(lambda y, xl, z, xh, k: (y, xl, (z - 1) % 4, xh, k))
CORE = pairs_of(lambda y, xl, z, xh, k: (y, xl, z, xh, 1 - k))


def send(value, pairs):
    return lax.ppermute(value, MESH_AXES, pairs)


def both_cores(*steps):
    return [(dz, dx, k, h) for k in (0, 1) for dz, dx in steps for h in (0, 1)]


FIRST = both_cores((0, 0), (0, 1), (-1, 0), (1, 0))
LATER = ((-1, 1), (1, 1), (2, 1))
SECOND = both_cores((2, 0)) + both_cores(*LATER)[: 2 * len(LATER)]
THIRD = both_cores(*LATER)[2 * len(LATER) :]
ORDER = np.array(FIRST + SECOND + THIRD, np.int32)


def half_index(col, entry):
    dz, dx, dk, half = ORDER[entry].tolist()
    z = (col // 4 + dz) % 4
    xh = (col // 2 + dx) % 2
    k = (col + dk) % 2
    return (z * 4 + xh * 2 + k) * 2 + half


ROWS = pl.BlockSpec(memory_space=pltpu.VMEM)
FAR = pl.BlockSpec(memory_space=pltpu.HBM)
WORDS = pl.BlockSpec(memory_space=pltpu.SMEM)


def near(value):
    return pltpu.with_memory_space_constraint(value, pltpu.VMEM)


def far(value):
    return pltpu.with_memory_space_constraint(value, pltpu.HBM)


def params(mib):
    return pltpu.CompilerParams(vmem_limit_bytes=mib * MIB)


def cost(flops, nbytes):
    return pl.CostEstimate(flops=2 * flops, transcendentals=0, bytes_accessed=2 * nbytes)


def product(left, right):
    return jnp.dot(left, right, preferred_element_type=jnp.float32)


def message_kernel(
    count_ref, rows_hbm, weight_hbm, feats_hbm, out_ref, rows_ref, weight_ref, feats_ref,
    stage_ref, load_sems, sems,
):
    sources = (rows_hbm, weight_hbm, feats_hbm)
    targets = (rows_ref, weight_ref, feats_ref)
    loads = [
        pltpu.make_async_copy(source, target, load_sems.at[i])
        for i, (source, target) in enumerate(zip(sources, targets))
    ]
    for load in loads:
        load.start()
    loads[0].wait()
    loads[1].wait()
    slot = lax.broadcasted_iota(jnp.int32, (1, SLOTS), 1)
    kept = [
        jnp.where(slot < count_ref[d], weight_ref[d : d + 1, :].astype(jnp.float32), 0.0)
        for d in range(8)
    ]
    kept = jnp.concatenate(kept, axis=0)
    kept_t = jnp.transpose(kept)
    rows_t = jnp.transpose(rows_ref[...])
    node = lax.broadcasted_iota(jnp.int32, (SLOTS, NODES), 1)
    copies = []
    for pair in range(4):
        hot = [
            jnp.where(rows_t[:, d : d + 1] == node, 1.0, 0.0).astype(jnp.bfloat16)
            for d in (2 * pair, 2 * pair + 1)
        ]
        if pair == 0:
            loads[2].wait()
        picked = product(jnp.concatenate(hot, axis=0), feats_ref[...])
        for q in range(2):
            d = 2 * pair + q
            block = picked[q * SLOTS : (q + 1) * SLOTS, :] * kept_t[:, d : d + 1]
            stage_ref[d, 0:SLOTS, :] = block.astype(jnp.bfloat16)
            line = jnp.broadcast_to(kept[d : d + 1, :], (PAD, SLOTS)).astype(jnp.bfloat16)
            stage_ref[d, SLOTS : SLOTS + PAD, 0:SLOTS] = line
            stage_ref[d, SLOTS : SLOTS + PAD, SLOTS:] = jnp.zeros(
                (PAD, D - SLOTS), jnp.bfloat16
            )
            copy = pltpu.make_async_copy(stage_ref.at[d], out_ref.at[d], sems.at[d])
            copy.start()
            copies.append(copy)
    for copy in copies:
        copy.wait()


def messages(node_feats, send_rows, send_count, send_weight):
    return pl.pallas_call(
        message_kernel,
        in_specs=[WORDS, FAR, FAR, FAR],
        out_specs=FAR,
        out_shape=pltpu.HBM((8, SLOTS + PAD, D), jnp.bfloat16),
        scratch_shapes=[
            pltpu.VMEM((8, SLOTS), jnp.int32),
            pltpu.VMEM((8, SLOTS), jnp.bfloat16),
            pltpu.VMEM((NODES, D), jnp.bfloat16),
            pltpu.VMEM((8, SLOTS + PAD, D), jnp.bfloat16),
            pltpu.SemaphoreType.DMA((3,)),
            pltpu.SemaphoreType.DMA((8,)),
        ],
        compiler_params=params(12),
        cost_estimate=cost(2 * NODES * NODES * D, 5 * MIB),
        name="messages",
    )(send_count.reshape(8), far(send_rows), far(send_weight), far(node_feats))


FIRST_HALVES = len(FIRST)
LATER_HALVES = len(SECOND) + len(THIRD)


def place_kernel(
    blocks_ref, tiles_ref, early_ref, later_ref, sums_ref, stage_ref, tally_ref, sems
):
    col = lax.axis_index("col")
    tally_ref[...] = jnp.zeros_like(tally_ref)
    stage_ref[...] = jnp.zeros_like(stage_ref)
    early_ref[...] = jnp.zeros_like(early_ref)

    def place(p, ref, column):
        first = half_index(col, p) * 4
        for t in range(4):
            at = pl.multiple_of(blocks_ref[first + t] * TB, TB)
            tile = tiles_ref[first + t]
            ref[pl.ds(at, TB), column * TB : (column + 1) * TB] = tile
            tally_ref[pl.ds(at, TB), :] += tile.astype(jnp.float32)

    for p in range(LATER_HALVES):
        place(FIRST_HALVES + p, stage_ref, p)
    copies = [pltpu.make_async_copy(stage_ref, later_ref, sems.at[0])]
    copies[0].start()
    for p in range(FIRST_HALVES):
        place(p, early_ref, p)
    copies.append(pltpu.make_async_copy(tally_ref, sums_ref, sems.at[1]))
    copies[1].start()
    for copy in copies:
        copy.wait()


def placed_tiles(tile_blocks, tile_weights):
    return pl.pallas_call(
        place_kernel,
        in_specs=[WORDS, ROWS],
        out_specs=[ROWS, FAR, FAR],
        out_shape=[
            pltpu.VMEM((NODES, FIRST_HALVES * TB), jnp.bfloat16),
            pltpu.HBM((NODES, LATER_HALVES * TB), jnp.bfloat16),
            pltpu.HBM((NODES, TB), jnp.float32),
        ],
        scratch_shapes=[
            pltpu.VMEM((NODES, LATER_HALVES * TB), jnp.bfloat16),
            pltpu.VMEM((NODES, TB), jnp.float32),
            pltpu.SemaphoreType.DMA((2,)),
        ],
        compiler_params=params(8),
        cost_estimate=cost(0, 12 * MIB),
        name="placed_tiles",
    )(tile_blocks.reshape(128), near(tile_weights))


def bias_kernel(bias_ref, out_ref):
    out_ref[...] = jnp.broadcast_to(bias_ref[...], (8, D))


def bias_rows(out_bias):
    return pl.pallas_call(
        bias_kernel,
        in_specs=[ROWS],
        out_specs=ROWS,
        out_shape=pltpu.VMEM((8, D), jnp.float32),
        compiler_params=params(2),
        cost_estimate=cost(1000, 1000),
        name="bias_rows",
    )(near(out_bias.reshape(1, D)))


def self_kernel(feats_ref, weight_ref, bias_ref, out_ref, stage_ref, sems):
    copies = []
    for step in range(4):
        lanes = slice(step * 256, (step + 1) * 256)
        stage_ref[:, lanes] = (
            product(feats_ref[...], weight_ref[:, lanes]) + bias_ref[0:1, lanes]
        )
        copy = pltpu.make_async_copy(
            stage_ref.at[:, lanes], out_ref.at[:, lanes], sems.at[step]
        )
        copy.start()
        copies.append(copy)
    for copy in copies:
        copy.wait()


def self_part(node_feats, self_weight, bias):
    return pl.pallas_call(
        self_kernel,
        in_specs=[ROWS, ROWS, ROWS],
        out_specs=FAR,
        out_shape=pltpu.HBM((NODES, D), jnp.float32),
        scratch_shapes=[
            pltpu.VMEM((NODES, D), jnp.float32),
            pltpu.SemaphoreType.DMA((4,)),
        ],
        compiler_params=params(8),
        cost_estimate=cost(1000, 1000),
        name="self_part",
    )(near(node_feats), near(self_weight), near(bias))


def hub_products(placed, parts):
    width = sum(part.shape[0] for part in parts)

    def body(placed_ref, *refs):
        out_ref, stage_ref, sems = refs[-3:]
        copies = []
        for step in range(4):
            lanes = slice(step * 256, (step + 1) * 256)
            hubs = jnp.concatenate([ref[:, lanes] for ref in refs[: len(parts)]], axis=0)
            stage_ref[:, lanes] = product(placed_ref[:, :width], hubs)
            copy = pltpu.make_async_copy(
                stage_ref.at[:, lanes], out_ref.at[:, lanes], sems.at[step]
            )
            copy.start()
            copies.append(copy)
        for copy in copies:
            copy.wait()

    return pl.pallas_call(
        body,
        in_specs=[ROWS] * (1 + len(parts)),
        out_specs=FAR,
        out_shape=pltpu.HBM((NODES, D), jnp.float32),
        scratch_shapes=[pltpu.VMEM((NODES, D), jnp.float32), pltpu.SemaphoreType.DMA((4,))],
        compiler_params=params(10),
        cost_estimate=cost(2 * NODES * width * D, 10 * MIB),
        name="hub_products",
    )(near(placed), *[near(part) for part in parts])


def tail_part(sums, carry, arrive_node, arrived):
    def body(
        at_ref, got_ref, sums_hbm, carry_hbm, out_ref, scale_ref, hot_ref, sums_ref,
        carry_ref, sems,
    ):
        pairs = [(sums_hbm, sums_ref)]
        for step in range(4):
            lanes = slice(step * 256, (step + 1) * 256)
            pairs.append((carry_hbm.at[:, lanes], carry_ref.at[:, lanes]))
        loads = [
            pltpu.make_async_copy(source, target, sems.at[i])
            for i, (source, target) in enumerate(pairs)
        ]
        for load in loads:
            load.start()
        loads[0].wait()
        for step in range(4):
            rows = slice(step * 256, (step + 1) * 256)
            node = lax.broadcasted_iota(jnp.int32, (256, SLOTS), 0) + step * 256
            weights = sums_ref[rows, :]
            for o in range(8):
                hit = at_ref[o : o + 1, :] == node
                hot_ref[rows, o * SLOTS : (o + 1) * SLOTS] = jnp.where(hit, 1.0, 0.0).astype(
                    jnp.bfloat16
                )
                line = got_ref[o, SLOTS : SLOTS + 1, 0:SLOTS].astype(jnp.float32)
                weights = weights + jnp.where(hit, line, 0.0)
            weight_sum = jnp.sum(weights, axis=-1, keepdims=True)
            scale_ref[rows, :] = jnp.broadcast_to(lax.rsqrt(1.0 + weight_sum), (256, TB))
        for load in loads[1:]:
            load.wait()
        for step in range(4):
            lanes = slice(step * 256, (step + 1) * 256)
            got = jnp.concatenate([got_ref[o, 0:SLOTS, lanes] for o in range(8)], axis=0)
            out_ref[:, lanes] = product(hot_ref[...], got) + carry_ref[:, lanes]

    return pl.pallas_call(
        body,
        in_specs=[ROWS] * 2 + [FAR] * 2,
        out_specs=[ROWS, ROWS],
        out_shape=[pltpu.VMEM((NODES, D), jnp.float32), pltpu.VMEM((NODES, TB), jnp.float32)],
        scratch_shapes=[
            pltpu.VMEM((NODES, 8 * SLOTS), jnp.bfloat16),
            pltpu.VMEM((NODES, TB), jnp.float32),
            pltpu.VMEM((NODES, D), jnp.float32),
            pltpu.SemaphoreType.DMA((5,)),
        ],
        compiler_params=params(14),
        cost_estimate=cost(2 * NODES * NODES * D, 10 * MIB),
        name="tail_part",
    )(near(arrive_node), near(arrived), far(sums), far(carry))


def middle_part(placed, parts, carry):
    width = sum(part.shape[0] for part in parts)

    def body(placed_ref, carry_ref, *refs):
        for step in range(4):
            lanes = slice(step * 256, (step + 1) * 256)
            hubs = jnp.concatenate([ref[:, lanes] for ref in refs[: len(parts)]], axis=0)
            refs[-1][:, lanes] = product(placed_ref[:, 0:width], hubs) + carry_ref[:, lanes]

    return pl.pallas_call(
        body,
        in_specs=[ROWS] * (2 + len(parts)),
        out_specs=ROWS,
        out_shape=pltpu.VMEM((NODES, D), jnp.float32),
        compiler_params=params(8),
        cost_estimate=cost(2 * NODES * width * D, 10 * MIB),
        name="middle_part",
    )(near(placed), near(carry), *[near(part) for part in parts])


def last_part(placed, parts, scale, carry, base, neigh_weight):
    tm = 256

    width = sum(part.shape[0] for part in parts)
    first = placed.shape[1] - width

    def body(scale_ref, carry_ref, base_ref, weight_ref, placed_ref, *refs):
        out_ref, stage_ref, sems = refs[len(parts) :]
        copies = []
        for step in range(NODES // tm):
            rows = slice(step * tm, (step + 1) * tm)
            hubs = jnp.concatenate([ref[...] for ref in refs[: len(parts)]], axis=0)
            combined = carry_ref[rows, :] + product(placed_ref[rows, first:], hubs)
            neighbour = (combined * scale_ref[rows, 0:1]).astype(jnp.bfloat16)
            preact = base_ref[rows, :] + product(neighbour, weight_ref[...])
            hidden = jnp.maximum(preact, 0.0)
            norm = lax.rsqrt(jnp.mean(hidden * hidden, axis=-1, keepdims=True) + 1e-06)
            stage_ref[rows, :] = (hidden * norm).astype(jnp.bfloat16)
            copy = pltpu.make_async_copy(
                stage_ref.at[rows], out_ref.at[rows], sems.at[step]
            )
            copy.start()
            copies.append(copy)
        for copy in copies:
            copy.wait()

    return pl.pallas_call(
        body,
        in_specs=[ROWS] * (5 + len(parts)),
        out_specs=FAR,
        out_shape=pltpu.HBM((NODES, D), jnp.bfloat16),
        scratch_shapes=[
            pltpu.VMEM((NODES, D), jnp.bfloat16),
            pltpu.SemaphoreType.DMA((NODES // tm,)),
        ],
        compiler_params=params(12),
        cost_estimate=cost(2 * NODES * D * (width + D), 16 * MIB),
        name="last_part",
    )(
        *[near(value) for value in (scale, carry, base, neigh_weight, placed, *parts)],
    )


def shards(
    node_feats,
    hub_feats,
    self_weight,
    neigh_weight,
    out_bias,
    tile_weights,
    tile_blocks,
    send_rows,
    send_count,
    send_weight,
    arrive_node,
):
    own = hub_feats
    across = send(own, ACROSS)
    up = send(own, UP)
    down = send(own, DOWN)

    message = messages(node_feats, send_rows, send_count, send_weight)

    out_bias, own_k, message = lax.optimization_barrier((out_bias, own, message))
    arrived = lax.all_to_all(message, "row", split_axis=0, concat_axis=0, tiled=True)
    own_c = send(own_k, CORE)
    bias = bias_rows(out_bias)
    up, down, across, own_c, bias = lax.optimization_barrier((up, down, across, own_c, bias))
    two_low = send(up[:TB], UP)
    two_high = send(down[TB:], DOWN)
    across_c = send(across, CORE)
    up_c = send(up, CORE)
    down_c = send(down, CORE)
    placed, placed_later, sums = placed_tiles(tile_blocks, tile_weights)

    base = self_part(node_feats, self_weight, bias)

    two_low, two_high, across, across_c, up_c, down_c, placed, base = (
        lax.optimization_barrier(
            (two_low, two_high, across, across_c, up_c, down_c, placed, base)
        )
    )
    two = jnp.concatenate([two_low, two_high], 0)
    up_x = send(across, UP)
    down_x = send(across, DOWN)
    two_x = send(two, ACROSS)
    two_c = send(two, CORE)
    carry = hub_products(
        placed, [own, across, up, down, own_c, across_c, up_c, down_c]
    )

    carry, scale = tail_part(sums, carry, arrive_node, arrived)

    up_x, down_x, two_x, two_c, carry = lax.optimization_barrier(
        (up_x, down_x, two_x, two_c, carry)
    )
    late = [send(part, CORE) for part in (up_x, down_x, two_x)]
    carry = middle_part(placed_later, [two, two_c, up_x, down_x, two_x], carry)
    return last_part(placed_later, late, scale, carry, base, neigh_weight)


def solution(mesh):
    placed = (
        P(("row", "col"), None),
        P("col", None),
        P(),
        P(),
        P(),
        P(("row", "col"), None, None),
        P(("row", "col"), None),
        P("row", "col"),
        P("row", "col"),
        P("row", "col"),
        P("row", "col"),
    )
    return jax.shard_map(
        shards, mesh=mesh, in_specs=placed, out_specs=P(("row", "col"), None), check_vma=False
    )
```

```python
import numpy as np
import jax
import jax.numpy as jnp
from jax import lax
from jax.experimental import pallas as pl
from jax.experimental.pallas import tpu as pltpu
from jax.sharding import PartitionSpec as P

MESH_AXES = ("row", "col")
D = 1024
TB = 128
NODES = 1024
SLOTS = 128
PAD = 8
MIB = 1 << 20


def flat(y, xl, z, xh, k):
    return (y * 2 + xl) * 16 + z * 4 + xh * 2 + k


def pairs_of(move):
    pairs = []
    for source in range(128):
        row, col = divmod(source, 16)
        place = (row // 2, row % 2, col // 4, (col // 2) % 2, col % 2)
        pairs.append((source, flat(*move(*place))))
    return pairs


ACROSS = pairs_of(lambda y, xl, z, xh, k: (y, 1 - xl, z, 1 - xh, k))
UP = pairs_of(lambda y, xl, z, xh, k: (y, xl, (z + 1) % 4, xh, k))
DOWN = pairs_of(lambda y, xl, z, xh, k: (y, xl, (z - 1) % 4, xh, k))
ONWARD = pairs_of(lambda y, xl, z, xh, k: (y, xl, (z + 1 - 2 * k) % 4, xh, k))
CORE = pairs_of(lambda y, xl, z, xh, k: (y, xl, z, xh, 1 - k))


def send(value, pairs):
    return lax.ppermute(value, MESH_AXES, pairs)


def both_cores(*steps):
    return [(dz, dx, k, h) for k in (0, 1) for dz, dx in steps for h in (0, 1)]


FIRST = both_cores((0, 0), (0, 1), (-1, 0), (1, 0))
LATER = ((-1, 1), (1, 1), (2, 1))
SECOND = both_cores((2, 0)) + both_cores(*LATER)[: 2 * len(LATER)]
THIRD = both_cores(*LATER)[2 * len(LATER) :]
ORDER = np.array(FIRST + SECOND + THIRD, np.int32)


def half_index(col, entry):
    dz, dx, dk, half = ORDER[entry].tolist()
    z = (col // 4 + dz) % 4
    xh = (col // 2 + dx) % 2
    k = (col + dk) % 2
    return (z * 4 + xh * 2 + k) * 2 + half


ROWS = pl.BlockSpec(memory_space=pltpu.VMEM)
FAR = pl.BlockSpec(memory_space=pltpu.HBM)
WORDS = pl.BlockSpec(memory_space=pltpu.SMEM)


def near(value):
    return pltpu.with_memory_space_constraint(value, pltpu.VMEM)


def far(value):
    return pltpu.with_memory_space_constraint(value, pltpu.HBM)


def params(mib):
    return pltpu.CompilerParams(vmem_limit_bytes=mib * MIB)


def cost(flops, nbytes):
    return pl.CostEstimate(flops=2 * flops, transcendentals=0, bytes_accessed=2 * nbytes)


def product(left, right):
    return jnp.dot(left, right, preferred_element_type=jnp.float32)


def message_kernel(
    count_ref, rows_hbm, weight_hbm, feats_hbm, out_ref, rows_ref, weight_ref, feats_ref,
    stage_ref, load_sems, sems,
):
    sources = (rows_hbm, weight_hbm, feats_hbm)
    targets = (rows_ref, weight_ref, feats_ref)
    loads = [
        pltpu.make_async_copy(source, target, load_sems.at[i])
        for i, (source, target) in enumerate(zip(sources, targets))
    ]
    for load in loads:
        load.start()
    loads[0].wait()
    loads[1].wait()
    slot = lax.broadcasted_iota(jnp.int32, (1, SLOTS), 1)
    kept = [
        jnp.where(slot < count_ref[d], weight_ref[d : d + 1, :].astype(jnp.float32), 0.0)
        for d in range(8)
    ]
    kept = jnp.concatenate(kept, axis=0)
    kept_t = jnp.transpose(kept)
    rows_t = jnp.transpose(rows_ref[...])
    node = lax.broadcasted_iota(jnp.int32, (SLOTS, NODES), 1)
    copies = []
    for pair in range(4):
        hot = [
            jnp.where(rows_t[:, d : d + 1] == node, 1.0, 0.0).astype(jnp.bfloat16)
            for d in (2 * pair, 2 * pair + 1)
        ]
        if pair == 0:
            loads[2].wait()
        picked = product(jnp.concatenate(hot, axis=0), feats_ref[...])
        for q in range(2):
            d = 2 * pair + q
            block = picked[q * SLOTS : (q + 1) * SLOTS, :] * kept_t[:, d : d + 1]
            stage_ref[d, 0:SLOTS, :] = block.astype(jnp.bfloat16)
            line = jnp.broadcast_to(kept[d : d + 1, :], (PAD, SLOTS)).astype(jnp.bfloat16)
            stage_ref[d, SLOTS : SLOTS + PAD, 0:SLOTS] = line
            stage_ref[d, SLOTS : SLOTS + PAD, SLOTS:] = jnp.zeros(
                (PAD, D - SLOTS), jnp.bfloat16
            )
            copy = pltpu.make_async_copy(stage_ref.at[d], out_ref.at[d], sems.at[d])
            copy.start()
            copies.append(copy)
    for copy in copies:
        copy.wait()


def messages(node_feats, send_rows, send_count, send_weight):
    return pl.pallas_call(
        message_kernel,
        in_specs=[WORDS, FAR, FAR, FAR],
        out_specs=FAR,
        out_shape=pltpu.HBM((8, SLOTS + PAD, D), jnp.bfloat16),
        scratch_shapes=[
            pltpu.VMEM((8, SLOTS), jnp.int32),
            pltpu.VMEM((8, SLOTS), jnp.bfloat16),
            pltpu.VMEM((NODES, D), jnp.bfloat16),
            pltpu.VMEM((8, SLOTS + PAD, D), jnp.bfloat16),
            pltpu.SemaphoreType.DMA((3,)),
            pltpu.SemaphoreType.DMA((8,)),
        ],
        compiler_params=params(12),
        cost_estimate=cost(2 * NODES * NODES * D, 5 * MIB),
        name="messages",
    )(send_count.reshape(8), far(send_rows), far(send_weight), far(node_feats))


FIRST_HALVES = len(FIRST)
LATER_HALVES = len(SECOND) + len(THIRD)


def place_kernel(
    blocks_ref, tiles_ref, early_ref, later_ref, sums_ref, stage_ref, tally_ref, sems
):
    col = lax.axis_index("col")
    tally_ref[...] = jnp.zeros_like(tally_ref)
    stage_ref[...] = jnp.zeros_like(stage_ref)
    early_ref[...] = jnp.zeros_like(early_ref)

    def place(p, ref, column):
        first = half_index(col, p) * 4
        for t in range(4):
            at = pl.multiple_of(blocks_ref[first + t] * TB, TB)
            tile = tiles_ref[first + t]
            ref[pl.ds(at, TB), column * TB : (column + 1) * TB] = tile
            tally_ref[pl.ds(at, TB), :] += tile.astype(jnp.float32)

    for p in range(LATER_HALVES):
        place(FIRST_HALVES + p, stage_ref, p)
    copies = [pltpu.make_async_copy(stage_ref, later_ref, sems.at[0])]
    copies[0].start()
    for p in range(FIRST_HALVES):
        place(p, early_ref, p)
    copies.append(pltpu.make_async_copy(tally_ref, sums_ref, sems.at[1]))
    copies[1].start()
    for copy in copies:
        copy.wait()


def placed_tiles(tile_blocks, tile_weights):
    return pl.pallas_call(
        place_kernel,
        in_specs=[WORDS, ROWS],
        out_specs=[ROWS, FAR, FAR],
        out_shape=[
            pltpu.VMEM((NODES, FIRST_HALVES * TB), jnp.bfloat16),
            pltpu.HBM((NODES, LATER_HALVES * TB), jnp.bfloat16),
            pltpu.HBM((NODES, TB), jnp.float32),
        ],
        scratch_shapes=[
            pltpu.VMEM((NODES, LATER_HALVES * TB), jnp.bfloat16),
            pltpu.VMEM((NODES, TB), jnp.float32),
            pltpu.SemaphoreType.DMA((2,)),
        ],
        compiler_params=params(8),
        cost_estimate=cost(0, 12 * MIB),
        name="placed_tiles",
    )(tile_blocks.reshape(128), near(tile_weights))


def bias_kernel(bias_ref, out_ref):
    out_ref[...] = jnp.broadcast_to(bias_ref[...], (8, D))


def bias_rows(out_bias):
    return pl.pallas_call(
        bias_kernel,
        in_specs=[ROWS],
        out_specs=ROWS,
        out_shape=pltpu.VMEM((8, D), jnp.float32),
        compiler_params=params(2),
        cost_estimate=cost(1000, 1000),
        name="bias_rows",
    )(near(out_bias.reshape(1, D)))


def choose_kernel(up_ref, down_ref, out_ref):
    core = lax.axis_index("col") % 2

    @pl.when(core == 0)
    def _():
        out_ref[...] = up_ref[...]

    @pl.when(core == 1)
    def _():
        out_ref[...] = down_ref[...]


def choose(up, down):
    return pl.pallas_call(
        choose_kernel,
        in_specs=[ROWS, ROWS],
        out_specs=ROWS,
        out_shape=pltpu.VMEM(up.shape, up.dtype),
        compiler_params=params(2),
        cost_estimate=cost(1000, 1000),
        name="choose",
    )(near(up), near(down))


def self_kernel(feats_ref, weight_ref, bias_ref, out_ref, stage_ref, sems):
    copies = []
    for step in range(4):
        lanes = slice(step * 256, (step + 1) * 256)
        stage_ref[:, lanes] = (
            product(feats_ref[...], weight_ref[:, lanes]) + bias_ref[0:1, lanes]
        )
        copy = pltpu.make_async_copy(
            stage_ref.at[:, lanes], out_ref.at[:, lanes], sems.at[step]
        )
        copy.start()
        copies.append(copy)
    for copy in copies:
        copy.wait()


def self_part(node_feats, self_weight, bias):
    return pl.pallas_call(
        self_kernel,
        in_specs=[ROWS, ROWS, ROWS],
        out_specs=FAR,
        out_shape=pltpu.HBM((NODES, D), jnp.float32),
        scratch_shapes=[
            pltpu.VMEM((NODES, D), jnp.float32),
            pltpu.SemaphoreType.DMA((4,)),
        ],
        compiler_params=params(8),
        cost_estimate=cost(1000, 1000),
        name="self_part",
    )(near(node_feats), near(self_weight), near(bias))


def hub_products(placed, parts):
    width = sum(part.shape[0] for part in parts)

    def body(placed_ref, *refs):
        out_ref, stage_ref, sems = refs[-3:]
        copies = []
        for step in range(4):
            lanes = slice(step * 256, (step + 1) * 256)
            hubs = jnp.concatenate([ref[:, lanes] for ref in refs[: len(parts)]], axis=0)
            stage_ref[:, lanes] = product(placed_ref[:, :width], hubs)
            copy = pltpu.make_async_copy(
                stage_ref.at[:, lanes], out_ref.at[:, lanes], sems.at[step]
            )
            copy.start()
            copies.append(copy)
        for copy in copies:
            copy.wait()

    return pl.pallas_call(
        body,
        in_specs=[ROWS] * (1 + len(parts)),
        out_specs=FAR,
        out_shape=pltpu.HBM((NODES, D), jnp.float32),
        scratch_shapes=[pltpu.VMEM((NODES, D), jnp.float32), pltpu.SemaphoreType.DMA((4,))],
        compiler_params=params(10),
        cost_estimate=cost(int(3 * NODES * width * D), 15 * MIB),
        name="hub_products",
    )(near(placed), *[near(part) for part in parts])


def tail_part(sums, carry, arrive_node, arrived):
    def body(
        at_ref, got_ref, sums_hbm, carry_hbm, out_ref, scale_ref, hot_ref, sums_ref,
        carry_ref, sems,
    ):
        pairs = [(sums_hbm, sums_ref)]
        for step in range(4):
            lanes = slice(step * 256, (step + 1) * 256)
            pairs.append((carry_hbm.at[:, lanes], carry_ref.at[:, lanes]))
        loads = [
            pltpu.make_async_copy(source, target, sems.at[i])
            for i, (source, target) in enumerate(pairs)
        ]
        for load in loads:
            load.start()
        loads[0].wait()
        for step in range(4):
            rows = slice(step * 256, (step + 1) * 256)
            node = lax.broadcasted_iota(jnp.int32, (256, SLOTS), 0) + step * 256
            weights = sums_ref[rows, :]
            for o in range(8):
                hit = at_ref[o : o + 1, :] == node
                hot_ref[rows, o * SLOTS : (o + 1) * SLOTS] = jnp.where(hit, 1.0, 0.0).astype(
                    jnp.bfloat16
                )
                line = got_ref[o, SLOTS : SLOTS + 1, 0:SLOTS].astype(jnp.float32)
                weights = weights + jnp.where(hit, line, 0.0)
            weight_sum = jnp.sum(weights, axis=-1, keepdims=True)
            scale_ref[rows, :] = jnp.broadcast_to(lax.rsqrt(1.0 + weight_sum), (256, TB))
        for load in loads[1:]:
            load.wait()
        for step in range(4):
            lanes = slice(step * 256, (step + 1) * 256)
            got = jnp.concatenate([got_ref[o, 0:SLOTS, lanes] for o in range(8)], axis=0)
            out_ref[:, lanes] = product(hot_ref[...], got) + carry_ref[:, lanes]

    return pl.pallas_call(
        body,
        in_specs=[ROWS] * 2 + [FAR] * 2,
        out_specs=[ROWS, ROWS],
        out_shape=[pltpu.VMEM((NODES, D), jnp.float32), pltpu.VMEM((NODES, TB), jnp.float32)],
        scratch_shapes=[
            pltpu.VMEM((NODES, 8 * SLOTS), jnp.bfloat16),
            pltpu.VMEM((NODES, TB), jnp.float32),
            pltpu.VMEM((NODES, D), jnp.float32),
            pltpu.SemaphoreType.DMA((5,)),
        ],
        compiler_params=params(14),
        cost_estimate=cost(2 * NODES * NODES * D, 10 * MIB),
        name="tail_part",
    )(near(arrive_node), near(arrived), far(sums), far(carry))


def middle_part(placed, parts, carry):
    width = sum(part.shape[0] for part in parts)

    def body(placed_ref, carry_ref, *refs):
        for step in range(4):
            lanes = slice(step * 256, (step + 1) * 256)
            hubs = jnp.concatenate([ref[:, lanes] for ref in refs[: len(parts)]], axis=0)
            refs[-1][:, lanes] = product(placed_ref[:, 0:width], hubs) + carry_ref[:, lanes]

    return pl.pallas_call(
        body,
        in_specs=[ROWS] * (2 + len(parts)),
        out_specs=ROWS,
        out_shape=pltpu.VMEM((NODES, D), jnp.float32),
        compiler_params=params(8),
        cost_estimate=cost(2 * NODES * width * D, 10 * MIB),
        name="middle_part",
    )(near(placed), near(carry), *[near(part) for part in parts])


def last_part(placed, parts, scale, carry, base, neigh_weight):
    tm = 256

    width = sum(part.shape[0] for part in parts)
    first = placed.shape[1] - width

    def body(scale_ref, carry_ref, base_ref, weight_ref, placed_ref, *refs):
        out_ref, stage_ref, sems = refs[len(parts) :]
        copies = []
        for step in range(NODES // tm):
            rows = slice(step * tm, (step + 1) * tm)
            hubs = jnp.concatenate([ref[...] for ref in refs[: len(parts)]], axis=0)
            combined = carry_ref[rows, :] + product(placed_ref[rows, first:], hubs)
            neighbour = (combined * scale_ref[rows, 0:1]).astype(jnp.bfloat16)
            preact = base_ref[rows, :] + product(neighbour, weight_ref[...])
            hidden = jnp.maximum(preact, 0.0)
            norm = lax.rsqrt(jnp.mean(hidden * hidden, axis=-1, keepdims=True) + 1e-06)
            stage_ref[rows, :] = (hidden * norm).astype(jnp.bfloat16)
            copy = pltpu.make_async_copy(
                stage_ref.at[rows], out_ref.at[rows], sems.at[step]
            )
            copy.start()
            copies.append(copy)
        for copy in copies:
            copy.wait()

    return pl.pallas_call(
        body,
        in_specs=[ROWS] * (5 + len(parts)),
        out_specs=FAR,
        out_shape=pltpu.HBM((NODES, D), jnp.bfloat16),
        scratch_shapes=[
            pltpu.VMEM((NODES, D), jnp.bfloat16),
            pltpu.SemaphoreType.DMA((NODES // tm,)),
        ],
        compiler_params=params(12),
        cost_estimate=cost(2 * NODES * D * (width + D), 16 * MIB),
        name="last_part",
    )(
        *[near(value) for value in (scale, carry, base, neigh_weight, placed, *parts)],
    )


def shards(
    node_feats,
    hub_feats,
    self_weight,
    neigh_weight,
    out_bias,
    tile_weights,
    tile_blocks,
    send_rows,
    send_count,
    send_weight,
    arrive_node,
):
    own = hub_feats
    across = send(own, ACROSS)
    up = send(own, UP)
    down = send(own, DOWN)

    message = messages(node_feats, send_rows, send_count, send_weight)

    out_bias, own_k, message = lax.optimization_barrier((out_bias, own, message))
    arrived = lax.all_to_all(message, "row", split_axis=0, concat_axis=0, tiled=True)
    own_c = send(own_k, CORE)
    bias = bias_rows(out_bias)
    up, down, across, own_c, bias = lax.optimization_barrier((up, down, across, own_c, bias))
    two = send(choose(up, down), ONWARD)
    across_c = send(across, CORE)
    up_c = send(up, CORE)
    down_c = send(down, CORE)
    placed, placed_later, sums = placed_tiles(tile_blocks, tile_weights)

    two, across, across_c, up_c, down_c, placed, bias = lax.optimization_barrier(
        (two, across, across_c, up_c, down_c, placed, bias)
    )
    up_x = send(across, UP)
    down_x = send(across, DOWN)
    two_x = send(two, ACROSS)
    two_c = send(two, CORE)
    carry = hub_products(
        placed, [own, across, up, down, own_c, across_c, up_c, down_c]
    )

    base = self_part(node_feats, self_weight, bias)
    carry, scale = tail_part(sums, carry, arrive_node, arrived)

    up_x, down_x, two_x, two_c, carry, base = lax.optimization_barrier(
        (up_x, down_x, two_x, two_c, carry, base)
    )
    late = [send(part, CORE) for part in (up_x, down_x, two_x)]
    carry = middle_part(placed_later, [two, two_c, up_x, down_x, two_x], carry)
    return last_part(placed_later, late, scale, carry, base, neigh_weight)


def solution(mesh):
    placed = (
        P(("row", "col"), None),
        P("col", None),
        P(),
        P(),
        P(),
        P(("row", "col"), None, None),
        P(("row", "col"), None),
        P("row", "col"),
        P("row", "col"),
        P("row", "col"),
        P("row", "col"),
    )
    return jax.shard_map(
        shards, mesh=mesh, in_specs=placed, out_specs=P(("row", "col"), None), check_vma=False
    )
```

```python
import numpy as np
import jax
import jax.numpy as jnp
from jax import lax
from jax.experimental import pallas as pl
from jax.experimental.pallas import tpu as pltpu
from jax.sharding import PartitionSpec as P

MESH_AXES = ("row", "col")
D = 1024
TB = 128
NODES = 1024
SLOTS = 128
PAD = 8
MIB = 1 << 20


def flat(y, xl, z, xh, k):
    return (y * 2 + xl) * 16 + z * 4 + xh * 2 + k


def pairs_of(move):
    pairs = []
    for source in range(128):
        row, col = divmod(source, 16)
        place = (row // 2, row % 2, col // 4, (col // 2) % 2, col % 2)
        pairs.append((source, flat(*move(*place))))
    return pairs


ACROSS = pairs_of(lambda y, xl, z, xh, k: (y, 1 - xl, z, 1 - xh, k))
UP = pairs_of(lambda y, xl, z, xh, k: (y, xl, (z + 1) % 4, xh, k))
DOWN = pairs_of(lambda y, xl, z, xh, k: (y, xl, (z - 1) % 4, xh, k))
ONWARD = pairs_of(lambda y, xl, z, xh, k: (y, xl, (z + 1 - 2 * k) % 4, xh, k))
CORE = pairs_of(lambda y, xl, z, xh, k: (y, xl, z, xh, 1 - k))


def send(value, pairs):
    return lax.ppermute(value, MESH_AXES, pairs)


def both_cores(*steps):
    return [(dz, dx, k, h) for k in (0, 1) for dz, dx in steps for h in (0, 1)]


FIRST = both_cores((0, 0), (0, 1), (-1, 0), (1, 0))
LATER = ((-1, 1), (1, 1), (2, 1))
SECOND = both_cores((2, 0)) + both_cores(*LATER)[: 2 * len(LATER)]
THIRD = both_cores(*LATER)[2 * len(LATER) :]
ORDER = np.array(FIRST + SECOND + THIRD, np.int32)


def half_index(col, entry):
    dz, dx, dk, half = ORDER[entry].tolist()
    z = (col // 4 + dz) % 4
    xh = (col // 2 + dx) % 2
    k = (col + dk) % 2
    return (z * 4 + xh * 2 + k) * 2 + half


ROWS = pl.BlockSpec(memory_space=pltpu.VMEM)
FAR = pl.BlockSpec(memory_space=pltpu.HBM)
WORDS = pl.BlockSpec(memory_space=pltpu.SMEM)


def near(value):
    return pltpu.with_memory_space_constraint(value, pltpu.VMEM)


def far(value):
    return pltpu.with_memory_space_constraint(value, pltpu.HBM)


def params(mib):
    return pltpu.CompilerParams(vmem_limit_bytes=mib * MIB)


def cost(flops, nbytes):
    return pl.CostEstimate(flops=2 * flops, transcendentals=0, bytes_accessed=2 * nbytes)


def product(left, right):
    return jnp.dot(left, right, preferred_element_type=jnp.float32)


def message_kernel(
    count_ref, rows_hbm, weight_hbm, feats_hbm, out_ref, rows_ref, weight_ref, feats_ref,
    stage_ref, load_sems, sems,
):
    sources = (rows_hbm, weight_hbm, feats_hbm)
    targets = (rows_ref, weight_ref, feats_ref)
    loads = [
        pltpu.make_async_copy(source, target, load_sems.at[i])
        for i, (source, target) in enumerate(zip(sources, targets))
    ]
    for load in loads:
        load.start()
    loads[0].wait()
    loads[1].wait()
    slot = lax.broadcasted_iota(jnp.int32, (1, SLOTS), 1)
    kept = [
        jnp.where(slot < count_ref[d], weight_ref[d : d + 1, :].astype(jnp.float32), 0.0)
        for d in range(8)
    ]
    kept = jnp.concatenate(kept, axis=0)
    kept_t = jnp.transpose(kept)
    rows_t = jnp.transpose(rows_ref[...])
    node = lax.broadcasted_iota(jnp.int32, (SLOTS, NODES), 1)
    copies = []
    for pair in range(4):
        hot = [
            jnp.where(rows_t[:, d : d + 1] == node, 1.0, 0.0).astype(jnp.bfloat16)
            for d in (2 * pair, 2 * pair + 1)
        ]
        if pair == 0:
            loads[2].wait()
        picked = product(jnp.concatenate(hot, axis=0), feats_ref[...])
        for q in range(2):
            d = 2 * pair + q
            block = picked[q * SLOTS : (q + 1) * SLOTS, :] * kept_t[:, d : d + 1]
            stage_ref[d, 0:SLOTS, :] = block.astype(jnp.bfloat16)
            line = jnp.broadcast_to(kept[d : d + 1, :], (PAD, SLOTS)).astype(jnp.bfloat16)
            stage_ref[d, SLOTS : SLOTS + PAD, 0:SLOTS] = line
            stage_ref[d, SLOTS : SLOTS + PAD, SLOTS:] = jnp.zeros(
                (PAD, D - SLOTS), jnp.bfloat16
            )
            copy = pltpu.make_async_copy(stage_ref.at[d], out_ref.at[d], sems.at[d])
            copy.start()
            copies.append(copy)
    for copy in copies:
        copy.wait()


def messages(node_feats, send_rows, send_count, send_weight):
    return pl.pallas_call(
        message_kernel,
        in_specs=[WORDS, FAR, FAR, FAR],
        out_specs=FAR,
        out_shape=pltpu.HBM((8, SLOTS + PAD, D), jnp.bfloat16),
        scratch_shapes=[
            pltpu.VMEM((8, SLOTS), jnp.int32),
            pltpu.VMEM((8, SLOTS), jnp.bfloat16),
            pltpu.VMEM((NODES, D), jnp.bfloat16),
            pltpu.VMEM((8, SLOTS + PAD, D), jnp.bfloat16),
            pltpu.SemaphoreType.DMA((3,)),
            pltpu.SemaphoreType.DMA((8,)),
        ],
        compiler_params=params(12),
        cost_estimate=cost(2 * NODES * NODES * D, 5 * MIB),
        name="messages",
    )(send_count.reshape(8), far(send_rows), far(send_weight), far(node_feats))


FIRST_HALVES = len(FIRST)
LATER_HALVES = len(SECOND) + len(THIRD)


def place_kernel(
    blocks_ref, tiles_ref, early_ref, later_ref, sums_ref, stage_ref, tally_ref, sems
):
    col = lax.axis_index("col")
    tally_ref[...] = jnp.zeros_like(tally_ref)
    stage_ref[...] = jnp.zeros_like(stage_ref)
    early_ref[...] = jnp.zeros_like(early_ref)

    def place(p, ref, column):
        first = half_index(col, p) * 4
        for t in range(4):
            at = pl.multiple_of(blocks_ref[first + t] * TB, TB)
            tile = tiles_ref[first + t]
            ref[pl.ds(at, TB), column * TB : (column + 1) * TB] = tile
            tally_ref[pl.ds(at, TB), :] += tile.astype(jnp.float32)

    for p in range(LATER_HALVES):
        place(FIRST_HALVES + p, stage_ref, p)
    copies = [pltpu.make_async_copy(stage_ref, later_ref, sems.at[0])]
    copies[0].start()
    for p in range(FIRST_HALVES):
        place(p, early_ref, p)
    copies.append(pltpu.make_async_copy(tally_ref, sums_ref, sems.at[1]))
    copies[1].start()
    for copy in copies:
        copy.wait()


def placed_tiles(tile_blocks, tile_weights):
    return pl.pallas_call(
        place_kernel,
        in_specs=[WORDS, ROWS],
        out_specs=[ROWS, FAR, FAR],
        out_shape=[
            pltpu.VMEM((NODES, FIRST_HALVES * TB), jnp.bfloat16),
            pltpu.HBM((NODES, LATER_HALVES * TB), jnp.bfloat16),
            pltpu.HBM((NODES, TB), jnp.float32),
        ],
        scratch_shapes=[
            pltpu.VMEM((NODES, LATER_HALVES * TB), jnp.bfloat16),
            pltpu.VMEM((NODES, TB), jnp.float32),
            pltpu.SemaphoreType.DMA((2,)),
        ],
        compiler_params=params(8),
        cost_estimate=cost(0, 12 * MIB),
        name="placed_tiles",
    )(tile_blocks.reshape(128), near(tile_weights))


def bias_kernel(bias_ref, out_ref):
    out_ref[...] = jnp.broadcast_to(bias_ref[...], (8, D))


def bias_rows(out_bias):
    return pl.pallas_call(
        bias_kernel,
        in_specs=[ROWS],
        out_specs=ROWS,
        out_shape=pltpu.VMEM((8, D), jnp.float32),
        compiler_params=params(2),
        cost_estimate=cost(1000, 1000),
        name="bias_rows",
    )(near(out_bias.reshape(1, D)))


def choose_kernel(up_ref, down_ref, out_ref):
    core = lax.axis_index("col") % 2

    @pl.when(core == 0)
    def _():
        out_ref[...] = up_ref[...]

    @pl.when(core == 1)
    def _():
        out_ref[...] = down_ref[...]


def choose(up, down):
    return pl.pallas_call(
        choose_kernel,
        in_specs=[ROWS, ROWS],
        out_specs=ROWS,
        out_shape=pltpu.VMEM(up.shape, up.dtype),
        compiler_params=params(2),
        cost_estimate=cost(1000, 1000),
        name="choose",
    )(near(up), near(down))


def self_kernel(feats_ref, weight_ref, bias_ref, out_ref, stage_ref, sems):
    copies = []
    for step in range(4):
        lanes = slice(step * 256, (step + 1) * 256)
        stage_ref[:, lanes] = (
            product(feats_ref[...], weight_ref[:, lanes]) + bias_ref[0:1, lanes]
        )
        copy = pltpu.make_async_copy(
            stage_ref.at[:, lanes], out_ref.at[:, lanes], sems.at[step]
        )
        copy.start()
        copies.append(copy)
    for copy in copies:
        copy.wait()


def self_part(node_feats, self_weight, bias):
    return pl.pallas_call(
        self_kernel,
        in_specs=[ROWS, ROWS, ROWS],
        out_specs=FAR,
        out_shape=pltpu.HBM((NODES, D), jnp.float32),
        scratch_shapes=[
            pltpu.VMEM((NODES, D), jnp.float32),
            pltpu.SemaphoreType.DMA((4,)),
        ],
        compiler_params=params(8),
        cost_estimate=cost(1000, 1000),
        name="self_part",
    )(near(node_feats), near(self_weight), near(bias))


def hub_products(placed, parts):
    width = sum(part.shape[0] for part in parts)

    def body(placed_ref, *refs):
        out_ref, stage_ref, sems = refs[-3:]
        copies = []
        for step in range(4):
            lanes = slice(step * 256, (step + 1) * 256)
            hubs = jnp.concatenate([ref[:, lanes] for ref in refs[: len(parts)]], axis=0)
            stage_ref[:, lanes] = product(placed_ref[:, :width], hubs)
            copy = pltpu.make_async_copy(
                stage_ref.at[:, lanes], out_ref.at[:, lanes], sems.at[step]
            )
            copy.start()
            copies.append(copy)
        for copy in copies:
            copy.wait()

    return pl.pallas_call(
        body,
        in_specs=[ROWS] * (1 + len(parts)),
        out_specs=FAR,
        out_shape=pltpu.HBM((NODES, D), jnp.float32),
        scratch_shapes=[pltpu.VMEM((NODES, D), jnp.float32), pltpu.SemaphoreType.DMA((4,))],
        compiler_params=params(10),
        cost_estimate=cost(int(3 * NODES * width * D), 15 * MIB),
        name="hub_products",
    )(near(placed), *[near(part) for part in parts])


def tail_part(sums, arrive_node, arrived):
    def body(at_ref, got_ref, sums_hbm, out_ref, scale_ref, hot_ref, sums_ref, sem):
        load = pltpu.make_async_copy(sums_hbm, sums_ref, sem)
        load.start()
        for step in range(4):
            rows = slice(step * 256, (step + 1) * 256)
            node = lax.broadcasted_iota(jnp.int32, (256, SLOTS), 0) + step * 256
            weights = jnp.zeros((256, SLOTS), jnp.float32)
            for o in range(8):
                hit = at_ref[o : o + 1, :] == node
                hot_ref[rows, o * SLOTS : (o + 1) * SLOTS] = jnp.where(hit, 1.0, 0.0).astype(
                    jnp.bfloat16
                )
                line = got_ref[o, SLOTS : SLOTS + 1, 0:SLOTS].astype(jnp.float32)
                weights = weights + jnp.where(hit, line, 0.0)
            scale_ref[rows, :] = weights
        load.wait()
        weight_sum = jnp.sum(scale_ref[...] + sums_ref[...], axis=-1, keepdims=True)
        scale_ref[...] = jnp.broadcast_to(lax.rsqrt(1.0 + weight_sum), (NODES, TB))
        for step in range(4):
            lanes = slice(step * 256, (step + 1) * 256)
            got = jnp.concatenate([got_ref[o, 0:SLOTS, lanes] for o in range(8)], axis=0)
            out_ref[:, lanes] = product(hot_ref[...], got)

    return pl.pallas_call(
        body,
        in_specs=[ROWS] * 2 + [FAR],
        out_specs=[ROWS, ROWS],
        out_shape=[pltpu.VMEM((NODES, D), jnp.float32), pltpu.VMEM((NODES, TB), jnp.float32)],
        scratch_shapes=[
            pltpu.VMEM((NODES, 8 * SLOTS), jnp.bfloat16),
            pltpu.VMEM((NODES, TB), jnp.float32),
            pltpu.SemaphoreType.DMA,
        ],
        compiler_params=params(10),
        cost_estimate=cost(2 * NODES * NODES * D, 10 * MIB),
        name="tail_part",
    )(near(arrive_node), near(arrived), far(sums))


def middle_part(placed, parts, carry, tail):
    width = sum(part.shape[0] for part in parts)

    def body(placed_ref, carry_ref, tail_ref, *refs):
        for step in range(4):
            lanes = slice(step * 256, (step + 1) * 256)
            hubs = jnp.concatenate([ref[:, lanes] for ref in refs[: len(parts)]], axis=0)
            total = product(placed_ref[:, 0:width], hubs) + carry_ref[:, lanes]
            refs[-1][:, lanes] = total + tail_ref[:, lanes]

    return pl.pallas_call(
        body,
        in_specs=[ROWS] * (3 + len(parts)),
        out_specs=ROWS,
        out_shape=pltpu.VMEM((NODES, D), jnp.float32),
        compiler_params=params(8),
        cost_estimate=cost(2 * NODES * width * D, 10 * MIB),
        name="middle_part",
    )(near(placed), near(carry), near(tail), *[near(part) for part in parts])


def last_part(placed, parts, scale, carry, base, neigh_weight):
    tm = 256

    width = sum(part.shape[0] for part in parts)
    first = placed.shape[1] - width

    def body(scale_ref, carry_ref, base_ref, weight_ref, placed_ref, *refs):
        out_ref, stage_ref, sems = refs[len(parts) :]
        copies = []
        for step in range(NODES // tm):
            rows = slice(step * tm, (step + 1) * tm)
            hubs = jnp.concatenate([ref[...] for ref in refs[: len(parts)]], axis=0)
            combined = carry_ref[rows, :] + product(placed_ref[rows, first:], hubs)
            neighbour = (combined * scale_ref[rows, 0:1]).astype(jnp.bfloat16)
            preact = base_ref[rows, :] + product(neighbour, weight_ref[...])
            hidden = jnp.maximum(preact, 0.0)
            norm = lax.rsqrt(jnp.mean(hidden * hidden, axis=-1, keepdims=True) + 1e-06)
            stage_ref[rows, :] = (hidden * norm).astype(jnp.bfloat16)
            copy = pltpu.make_async_copy(
                stage_ref.at[rows], out_ref.at[rows], sems.at[step]
            )
            copy.start()
            copies.append(copy)
        for copy in copies:
            copy.wait()

    return pl.pallas_call(
        body,
        in_specs=[ROWS] * (5 + len(parts)),
        out_specs=FAR,
        out_shape=pltpu.HBM((NODES, D), jnp.bfloat16),
        scratch_shapes=[
            pltpu.VMEM((NODES, D), jnp.bfloat16),
            pltpu.SemaphoreType.DMA((NODES // tm,)),
        ],
        compiler_params=params(12),
        cost_estimate=cost(2 * NODES * D * (width + D), 16 * MIB),
        name="last_part",
    )(
        *[near(value) for value in (scale, carry, base, neigh_weight, placed, *parts)],
    )


def shards(
    node_feats,
    hub_feats,
    self_weight,
    neigh_weight,
    out_bias,
    tile_weights,
    tile_blocks,
    send_rows,
    send_count,
    send_weight,
    arrive_node,
):
    own = hub_feats
    across = send(own, ACROSS)
    up = send(own, UP)
    down = send(own, DOWN)

    message = messages(node_feats, send_rows, send_count, send_weight)

    out_bias, own_k, message = lax.optimization_barrier((out_bias, own, message))
    arrived = lax.all_to_all(message, "row", split_axis=0, concat_axis=0, tiled=True)
    own_c = send(own_k, CORE)
    bias = bias_rows(out_bias)
    up, down, across, own_c, bias = lax.optimization_barrier((up, down, across, own_c, bias))
    two = send(choose(up, down), ONWARD)
    across_c = send(across, CORE)
    up_c = send(up, CORE)
    down_c = send(down, CORE)
    placed, placed_later, sums = placed_tiles(tile_blocks, tile_weights)

    two, across, across_c, up_c, down_c, placed, bias = lax.optimization_barrier(
        (two, across, across_c, up_c, down_c, placed, bias)
    )
    up_x = send(across, UP)
    down_x = send(across, DOWN)
    two_x = send(two, ACROSS)
    two_c = send(two, CORE)
    carry = hub_products(
        placed, [own, across, up, down, own_c, across_c, up_c, down_c]
    )

    base = self_part(node_feats, self_weight, bias)
    tail, scale = tail_part(sums, arrive_node, arrived)

    up_x, down_x, two_x, two_c, carry, tail, base = lax.optimization_barrier(
        (up_x, down_x, two_x, two_c, carry, tail, base)
    )
    late = [send(part, CORE) for part in (up_x, down_x, two_x)]
    carry = middle_part(placed_later, [two, two_c, up_x, down_x, two_x], carry, tail)
    return last_part(placed_later, late, scale, carry, base, neigh_weight)


def solution(mesh):
    placed = (
        P(("row", "col"), None),
        P("col", None),
        P(),
        P(),
        P(),
        P(("row", "col"), None, None),
        P(("row", "col"), None),
        P("row", "col"),
        P("row", "col"),
        P("row", "col"),
        P("row", "col"),
    )
    return jax.shard_map(
        shards, mesh=mesh, in_specs=placed, out_specs=P(("row", "col"), None), check_vma=False
    )
```

```python
import numpy as np
import jax
import jax.numpy as jnp
from jax import lax
from jax.experimental import pallas as pl
from jax.experimental.pallas import tpu as pltpu
from jax.sharding import PartitionSpec as P

MESH_AXES = ("row", "col")
D = 1024
TB = 128
NODES = 1024
SLOTS = 128
PAD = 8
MIB = 1 << 20


def flat(y, xl, z, xh, k):
    return (y * 2 + xl) * 16 + z * 4 + xh * 2 + k


def pairs_of(move):
    pairs = []
    for source in range(128):
        row, col = divmod(source, 16)
        place = (row // 2, row % 2, col // 4, (col // 2) % 2, col % 2)
        pairs.append((source, flat(*move(*place))))
    return pairs


ACROSS = pairs_of(lambda y, xl, z, xh, k: (y, 1 - xl, z, 1 - xh, k))
UP = pairs_of(lambda y, xl, z, xh, k: (y, xl, (z + 1) % 4, xh, k))
DOWN = pairs_of(lambda y, xl, z, xh, k: (y, xl, (z - 1) % 4, xh, k))
ONWARD = pairs_of(lambda y, xl, z, xh, k: (y, xl, (z + 1 - 2 * k) % 4, xh, k))
CORE = pairs_of(lambda y, xl, z, xh, k: (y, xl, z, xh, 1 - k))


def send(value, pairs):
    return lax.ppermute(value, MESH_AXES, pairs)


def both_cores(*steps):
    return [(dz, dx, k, h) for k in (0, 1) for dz, dx in steps for h in (0, 1)]


FIRST = both_cores((0, 0), (0, 1), (-1, 0), (1, 0))
LATER = ((-1, 1), (1, 1), (2, 1))
SECOND = both_cores((2, 0)) + both_cores(*LATER)[: 2 * len(LATER)]
THIRD = both_cores(*LATER)[2 * len(LATER) :]
ORDER = np.array(FIRST + SECOND + THIRD, np.int32)


def half_index(col, entry):
    dz, dx, dk, half = ORDER[entry].tolist()
    z = (col // 4 + dz) % 4
    xh = (col // 2 + dx) % 2
    k = (col + dk) % 2
    return (z * 4 + xh * 2 + k) * 2 + half


ROWS = pl.BlockSpec(memory_space=pltpu.VMEM)
FAR = pl.BlockSpec(memory_space=pltpu.HBM)
WORDS = pl.BlockSpec(memory_space=pltpu.SMEM)


def near(value):
    return pltpu.with_memory_space_constraint(value, pltpu.VMEM)


def far(value):
    return pltpu.with_memory_space_constraint(value, pltpu.HBM)


def params(mib):
    return pltpu.CompilerParams(vmem_limit_bytes=mib * MIB)


def cost(flops, nbytes):
    return pl.CostEstimate(flops=2 * flops, transcendentals=0, bytes_accessed=2 * nbytes)


def product(left, right):
    return jnp.dot(left, right, preferred_element_type=jnp.float32)


def message_kernel(
    count_ref, rows_hbm, weight_hbm, feats_hbm, out_ref, rows_ref, weight_ref, feats_ref,
    stage_ref, load_sems, sems,
):
    sources = (rows_hbm, weight_hbm, feats_hbm)
    targets = (rows_ref, weight_ref, feats_ref)
    loads = [
        pltpu.make_async_copy(source, target, load_sems.at[i])
        for i, (source, target) in enumerate(zip(sources, targets))
    ]
    for load in loads:
        load.start()
    loads[0].wait()
    loads[1].wait()
    slot = lax.broadcasted_iota(jnp.int32, (1, SLOTS), 1)
    kept = [
        jnp.where(slot < count_ref[d], weight_ref[d : d + 1, :].astype(jnp.float32), 0.0)
        for d in range(8)
    ]
    kept = jnp.concatenate(kept, axis=0)
    kept_t = jnp.transpose(kept)
    rows_t = jnp.transpose(rows_ref[...])
    node = lax.broadcasted_iota(jnp.int32, (SLOTS, NODES), 1)
    copies = []
    for pair in range(4):
        hot = [
            jnp.where(rows_t[:, d : d + 1] == node, 1.0, 0.0).astype(jnp.bfloat16)
            for d in (2 * pair, 2 * pair + 1)
        ]
        if pair == 0:
            loads[2].wait()
        picked = product(jnp.concatenate(hot, axis=0), feats_ref[...])
        for q in range(2):
            d = 2 * pair + q
            block = picked[q * SLOTS : (q + 1) * SLOTS, :] * kept_t[:, d : d + 1]
            stage_ref[d, 0:SLOTS, :] = block.astype(jnp.bfloat16)
            line = jnp.broadcast_to(kept[d : d + 1, :], (PAD, SLOTS)).astype(jnp.bfloat16)
            stage_ref[d, SLOTS : SLOTS + PAD, 0:SLOTS] = line
            stage_ref[d, SLOTS : SLOTS + PAD, SLOTS:] = jnp.zeros(
                (PAD, D - SLOTS), jnp.bfloat16
            )
            copy = pltpu.make_async_copy(stage_ref.at[d], out_ref.at[d], sems.at[d])
            copy.start()
            copies.append(copy)
    for copy in copies:
        copy.wait()


def messages(node_feats, send_rows, send_count, send_weight):
    return pl.pallas_call(
        message_kernel,
        in_specs=[WORDS, FAR, FAR, FAR],
        out_specs=FAR,
        out_shape=pltpu.HBM((8, SLOTS + PAD, D), jnp.bfloat16),
        scratch_shapes=[
            pltpu.VMEM((8, SLOTS), jnp.int32),
            pltpu.VMEM((8, SLOTS), jnp.bfloat16),
            pltpu.VMEM((NODES, D), jnp.bfloat16),
            pltpu.VMEM((8, SLOTS + PAD, D), jnp.bfloat16),
            pltpu.SemaphoreType.DMA((3,)),
            pltpu.SemaphoreType.DMA((8,)),
        ],
        compiler_params=params(12),
        cost_estimate=cost(2 * NODES * NODES * D, 5 * MIB),
        name="messages",
    )(far(send_count.reshape(8)), far(send_rows), far(send_weight), far(node_feats))


FIRST_HALVES = len(FIRST)
LATER_HALVES = len(SECOND) + len(THIRD)


def place_kernel(
    blocks_ref, tiles_ref, early_ref, later_ref, sums_ref, stage_ref, tally_ref, sems
):
    col = lax.axis_index("col")
    tally_ref[...] = jnp.zeros_like(tally_ref)
    stage_ref[...] = jnp.zeros_like(stage_ref)
    early_ref[...] = jnp.zeros_like(early_ref)

    def place(p, ref, column):
        first = half_index(col, p) * 4
        for t in range(4):
            at = pl.multiple_of(blocks_ref[first + t] * TB, TB)
            tile = tiles_ref[first + t]
            ref[pl.ds(at, TB), column * TB : (column + 1) * TB] = tile
            tally_ref[pl.ds(at, TB), :] += tile.astype(jnp.float32)

    for p in range(LATER_HALVES):
        place(FIRST_HALVES + p, stage_ref, p)
    copies = [pltpu.make_async_copy(stage_ref, later_ref, sems.at[0])]
    copies[0].start()
    for p in range(FIRST_HALVES):
        place(p, early_ref, p)
    copies.append(pltpu.make_async_copy(tally_ref, sums_ref, sems.at[1]))
    copies[1].start()
    for copy in copies:
        copy.wait()


def placed_tiles(tile_blocks, tile_weights):
    return pl.pallas_call(
        place_kernel,
        in_specs=[WORDS, ROWS],
        out_specs=[ROWS, FAR, FAR],
        out_shape=[
            pltpu.VMEM((NODES, FIRST_HALVES * TB), jnp.bfloat16),
            pltpu.HBM((NODES, LATER_HALVES * TB), jnp.bfloat16),
            pltpu.HBM((NODES, TB), jnp.float32),
        ],
        scratch_shapes=[
            pltpu.VMEM((NODES, LATER_HALVES * TB), jnp.bfloat16),
            pltpu.VMEM((NODES, TB), jnp.float32),
            pltpu.SemaphoreType.DMA((2,)),
        ],
        compiler_params=params(8),
        cost_estimate=cost(0, 12 * MIB),
        name="placed_tiles",
    )(tile_blocks.reshape(128), near(tile_weights))


def bias_kernel(bias_ref, out_ref):
    out_ref[...] = jnp.broadcast_to(bias_ref[...], (8, D))


def bias_rows(out_bias):
    return pl.pallas_call(
        bias_kernel,
        in_specs=[ROWS],
        out_specs=ROWS,
        out_shape=pltpu.VMEM((8, D), jnp.float32),
        compiler_params=params(2),
        cost_estimate=cost(1000, 1000),
        name="bias_rows",
    )(near(out_bias.reshape(1, D)))


def choose_kernel(up_ref, down_ref, out_ref):
    core = lax.axis_index("col") % 2

    @pl.when(core == 0)
    def _():
        out_ref[...] = up_ref[...]

    @pl.when(core == 1)
    def _():
        out_ref[...] = down_ref[...]


def choose(up, down):
    return pl.pallas_call(
        choose_kernel,
        in_specs=[ROWS, ROWS],
        out_specs=ROWS,
        out_shape=pltpu.VMEM(up.shape, up.dtype),
        compiler_params=params(2),
        cost_estimate=cost(1000, 1000),
        name="choose",
    )(near(up), near(down))


def self_kernel(feats_ref, weight_ref, bias_ref, out_ref, stage_ref, sems):
    copies = []
    for step in range(4):
        rows = slice(step * 256, (step + 1) * 256)
        stage_ref[rows, :] = product(feats_ref[rows, :], weight_ref[...]) + bias_ref[0:1, :]
        copy = pltpu.make_async_copy(
            stage_ref.at[rows], out_ref.at[rows], sems.at[step]
        )
        copy.start()
        copies.append(copy)
    for copy in copies:
        copy.wait()


def self_part(node_feats, self_weight, bias):
    return pl.pallas_call(
        self_kernel,
        in_specs=[ROWS, ROWS, ROWS],
        out_specs=FAR,
        out_shape=pltpu.HBM((NODES, D), jnp.float32),
        scratch_shapes=[
            pltpu.VMEM((NODES, D), jnp.float32),
            pltpu.SemaphoreType.DMA((4,)),
        ],
        compiler_params=params(8),
        cost_estimate=cost(1000, 1000),
        name="self_part",
    )(near(node_feats), near(self_weight), near(bias))


def hub_products(placed, parts):
    width = sum(part.shape[0] for part in parts)

    def body(placed_ref, *refs):
        out_ref, stage_ref, sems = refs[-3:]
        copies = []
        for step in range(4):
            rows = slice(step * 256, (step + 1) * 256)
            hubs = jnp.concatenate([ref[...] for ref in refs[: len(parts)]], axis=0)
            stage_ref[rows, :] = product(placed_ref[rows, :width], hubs)
            copy = pltpu.make_async_copy(
                stage_ref.at[rows], out_ref.at[rows], sems.at[step]
            )
            copy.start()
            copies.append(copy)
        for copy in copies:
            copy.wait()

    return pl.pallas_call(
        body,
        in_specs=[ROWS] * (1 + len(parts)),
        out_specs=FAR,
        out_shape=pltpu.HBM((NODES, D), jnp.float32),
        scratch_shapes=[pltpu.VMEM((NODES, D), jnp.float32), pltpu.SemaphoreType.DMA((4,))],
        compiler_params=params(16),
        cost_estimate=cost(int(3 * NODES * width * D), 15 * MIB),
        name="hub_products",
    )(near(placed), *[near(part) for part in parts])


def tail_part(sums, arrive_node, arrived):
    def body(at_ref, got_ref, sums_hbm, out_ref, scale_ref, hot_ref, sums_ref, sem):
        load = pltpu.make_async_copy(sums_hbm, sums_ref, sem)
        load.start()
        for step in range(4):
            rows = slice(step * 256, (step + 1) * 256)
            node = lax.broadcasted_iota(jnp.int32, (256, SLOTS), 0) + step * 256
            weights = jnp.zeros((256, SLOTS), jnp.float32)
            for o in range(8):
                hit = at_ref[o : o + 1, :] == node
                hot_ref[rows, o * SLOTS : (o + 1) * SLOTS] = jnp.where(hit, 1.0, 0.0).astype(
                    jnp.bfloat16
                )
                line = got_ref[o, SLOTS : SLOTS + 1, 0:SLOTS].astype(jnp.float32)
                weights = weights + jnp.where(hit, line, 0.0)
            scale_ref[rows, :] = weights
        load.wait()
        weight_sum = jnp.sum(scale_ref[...] + sums_ref[...], axis=-1, keepdims=True)
        scale_ref[...] = jnp.broadcast_to(lax.rsqrt(1.0 + weight_sum), (NODES, TB))
        for step in range(4):
            lanes = slice(step * 256, (step + 1) * 256)
            got = jnp.concatenate([got_ref[o, 0:SLOTS, lanes] for o in range(8)], axis=0)
            out_ref[:, lanes] = product(hot_ref[...], got)

    return pl.pallas_call(
        body,
        in_specs=[ROWS] * 2 + [FAR],
        out_specs=[ROWS, ROWS],
        out_shape=[pltpu.VMEM((NODES, D), jnp.float32), pltpu.VMEM((NODES, TB), jnp.float32)],
        scratch_shapes=[
            pltpu.VMEM((NODES, 8 * SLOTS), jnp.bfloat16),
            pltpu.VMEM((NODES, TB), jnp.float32),
            pltpu.SemaphoreType.DMA,
        ],
        compiler_params=params(10),
        cost_estimate=cost(2 * NODES * NODES * D, 10 * MIB),
        name="tail_part",
    )(near(arrive_node), near(arrived), far(sums))


def middle_part(placed, parts, carry, tail):
    width = sum(part.shape[0] for part in parts)

    def body(placed_ref, carry_ref, tail_ref, *refs):
        for step in range(4):
            lanes = slice(step * 256, (step + 1) * 256)
            hubs = jnp.concatenate([ref[:, lanes] for ref in refs[: len(parts)]], axis=0)
            total = product(placed_ref[:, 0:width], hubs) + carry_ref[:, lanes]
            refs[-1][:, lanes] = total + tail_ref[:, lanes]

    return pl.pallas_call(
        body,
        in_specs=[ROWS] * (3 + len(parts)),
        out_specs=ROWS,
        out_shape=pltpu.VMEM((NODES, D), jnp.float32),
        compiler_params=params(8),
        cost_estimate=cost(2 * NODES * width * D, 10 * MIB),
        name="middle_part",
    )(near(placed), near(carry), near(tail), *[near(part) for part in parts])


def last_part(placed, parts, scale, carry, base, neigh_weight):
    tm = 256

    width = sum(part.shape[0] for part in parts)
    first = placed.shape[1] - width

    def body(scale_ref, carry_ref, base_ref, weight_ref, placed_ref, *refs):
        out_ref, stage_ref, sems = refs[len(parts) :]
        copies = []
        for step in range(NODES // tm):
            rows = slice(step * tm, (step + 1) * tm)
            hubs = jnp.concatenate([ref[...] for ref in refs[: len(parts)]], axis=0)
            combined = carry_ref[rows, :] + product(placed_ref[rows, first:], hubs)
            neighbour = (combined * scale_ref[rows, 0:1]).astype(jnp.bfloat16)
            preact = base_ref[rows, :] + product(neighbour, weight_ref[...])
            hidden = jnp.maximum(preact, 0.0)
            norm = lax.rsqrt(jnp.mean(hidden * hidden, axis=-1, keepdims=True) + 1e-06)
            stage_ref[rows, :] = (hidden * norm).astype(jnp.bfloat16)
            copy = pltpu.make_async_copy(
                stage_ref.at[rows], out_ref.at[rows], sems.at[step]
            )
            copy.start()
            copies.append(copy)
        for copy in copies:
            copy.wait()

    return pl.pallas_call(
        body,
        in_specs=[ROWS] * (5 + len(parts)),
        out_specs=FAR,
        out_shape=pltpu.HBM((NODES, D), jnp.bfloat16),
        scratch_shapes=[
            pltpu.VMEM((NODES, D), jnp.bfloat16),
            pltpu.SemaphoreType.DMA((NODES // tm,)),
        ],
        compiler_params=params(12),
        cost_estimate=cost(2 * NODES * D * (width + D), 16 * MIB),
        name="last_part",
    )(
        *[near(value) for value in (scale, carry, base, neigh_weight, placed, *parts)],
    )


def shards(
    node_feats,
    hub_feats,
    self_weight,
    neigh_weight,
    out_bias,
    tile_weights,
    tile_blocks,
    send_rows,
    send_count,
    send_weight,
    arrive_node,
):
    own = hub_feats
    across = send(own, ACROSS)
    up = send(own, UP)
    down = send(own, DOWN)

    message = messages(node_feats, send_rows, send_count, send_weight)

    out_bias, own_k, message = lax.optimization_barrier((out_bias, own, message))
    arrived = lax.all_to_all(message, "row", split_axis=0, concat_axis=0, tiled=True)
    own_c = send(own_k, CORE)
    bias = bias_rows(out_bias)
    up, down, across, own_c, bias = lax.optimization_barrier((up, down, across, own_c, bias))
    two = send(choose(up, down), ONWARD)
    across_c = send(across, CORE)
    up_c = send(up, CORE)
    down_c = send(down, CORE)
    placed, placed_later, sums = placed_tiles(tile_blocks, tile_weights)

    two, across, across_c, up_c, down_c, placed, bias = lax.optimization_barrier(
        (two, across, across_c, up_c, down_c, placed, bias)
    )
    up_x = send(across, UP)
    down_x = send(across, DOWN)
    two_x = send(two, ACROSS)
    two_c = send(two, CORE)
    carry = hub_products(
        placed, [own, across, up, down, own_c, across_c, up_c, down_c]
    )

    base = self_part(node_feats, self_weight, bias)
    tail, scale = tail_part(sums, arrive_node, arrived)

    up_x, down_x, two_x, two_c, carry, tail, base = lax.optimization_barrier(
        (up_x, down_x, two_x, two_c, carry, tail, base)
    )
    late = [send(part, CORE) for part in (up_x, down_x, two_x)]
    carry = middle_part(placed_later, [two, two_c, up_x, down_x, two_x], carry, tail)
    return last_part(placed_later, late, scale, carry, base, neigh_weight)


def solution(mesh):
    placed = (
        P(("row", "col"), None),
        P("col", None),
        P(),
        P(),
        P(),
        P(("row", "col"), None, None),
        P(("row", "col"), None),
        P("row", "col"),
        P("row", "col"),
        P("row", "col"),
        P("row", "col"),
    )
    return jax.shard_map(
        shards, mesh=mesh, in_specs=placed, out_specs=P(("row", "col"), None), check_vma=False
    )
```

```python
import numpy as np
import jax
import jax.numpy as jnp
from jax import lax
from jax.experimental import pallas as pl
from jax.experimental.pallas import tpu as pltpu
from jax.sharding import PartitionSpec as P

MESH_AXES = ("row", "col")
D = 1024
TB = 128
NODES = 1024
SLOTS = 128
PAD = 8
MIB = 1 << 20


def flat(y, xl, z, xh, k):
    return (y * 2 + xl) * 16 + z * 4 + xh * 2 + k


def pairs_of(move):
    pairs = []
    for source in range(128):
        row, col = divmod(source, 16)
        place = (row // 2, row % 2, col // 4, (col // 2) % 2, col % 2)
        pairs.append((source, flat(*move(*place))))
    return pairs


ACROSS = pairs_of(lambda y, xl, z, xh, k: (y, 1 - xl, z, 1 - xh, k))
UP = pairs_of(lambda y, xl, z, xh, k: (y, xl, (z + 1) % 4, xh, k))
DOWN = pairs_of(lambda y, xl, z, xh, k: (y, xl, (z - 1) % 4, xh, k))
ONWARD = pairs_of(lambda y, xl, z, xh, k: (y, xl, (z + 1 - 2 * k) % 4, xh, k))
CORE = pairs_of(lambda y, xl, z, xh, k: (y, xl, z, xh, 1 - k))


def send(value, pairs):
    return lax.ppermute(value, MESH_AXES, pairs)


def both_cores(*steps):
    return [(dz, dx, k, h) for k in (0, 1) for dz, dx in steps for h in (0, 1)]


FIRST = both_cores((0, 0), (0, 1), (-1, 0), (1, 0))
LATER = ((-1, 1), (1, 1), (2, 1))
SECOND = both_cores((2, 0)) + both_cores(*LATER)[: 2 * len(LATER)]
THIRD = both_cores(*LATER)[2 * len(LATER) :]
ORDER = np.array(FIRST + SECOND + THIRD, np.int32)


def half_index(col, entry):
    dz, dx, dk, half = ORDER[entry].tolist()
    z = (col // 4 + dz) % 4
    xh = (col // 2 + dx) % 2
    k = (col + dk) % 2
    return (z * 4 + xh * 2 + k) * 2 + half


ROWS = pl.BlockSpec(memory_space=pltpu.VMEM)
FAR = pl.BlockSpec(memory_space=pltpu.HBM)
WORDS = pl.BlockSpec(memory_space=pltpu.SMEM)


def near(value):
    return pltpu.with_memory_space_constraint(value, pltpu.VMEM)


def far(value):
    return pltpu.with_memory_space_constraint(value, pltpu.HBM)


def params(mib):
    return pltpu.CompilerParams(vmem_limit_bytes=mib * MIB)


def cost(flops, nbytes):
    return pl.CostEstimate(flops=2 * flops, transcendentals=0, bytes_accessed=2 * nbytes)


def product(left, right):
    return jnp.dot(left, right, preferred_element_type=jnp.float32)


def message_kernel(
    count_ref, rows_hbm, weight_hbm, feats_hbm, out_ref, rows_ref, weight_ref, feats_ref,
    stage_ref, load_sems, sems,
):
    sources = (rows_hbm, weight_hbm, feats_hbm)
    targets = (rows_ref, weight_ref, feats_ref)
    loads = [
        pltpu.make_async_copy(source, target, load_sems.at[i])
        for i, (source, target) in enumerate(zip(sources, targets))
    ]
    for load in loads:
        load.start()
    loads[0].wait()
    loads[1].wait()
    slot = lax.broadcasted_iota(jnp.int32, (1, SLOTS), 1)
    kept = [
        jnp.where(slot < count_ref[d], weight_ref[d : d + 1, :].astype(jnp.float32), 0.0)
        for d in range(8)
    ]
    kept = jnp.concatenate(kept, axis=0)
    kept_t = jnp.transpose(kept)
    rows_t = jnp.transpose(rows_ref[...])
    node = lax.broadcasted_iota(jnp.int32, (SLOTS, NODES), 1)
    copies = []
    for pair in range(4):
        hot = [
            jnp.where(rows_t[:, d : d + 1] == node, 1.0, 0.0).astype(jnp.bfloat16)
            for d in (2 * pair, 2 * pair + 1)
        ]
        if pair == 0:
            loads[2].wait()
        picked = product(jnp.concatenate(hot, axis=0), feats_ref[...])
        for q in range(2):
            d = 2 * pair + q
            block = picked[q * SLOTS : (q + 1) * SLOTS, :] * kept_t[:, d : d + 1]
            stage_ref[d, 0:SLOTS, :] = block.astype(jnp.bfloat16)
            line = jnp.broadcast_to(kept[d : d + 1, :], (PAD, SLOTS)).astype(jnp.bfloat16)
            stage_ref[d, SLOTS : SLOTS + PAD, 0:SLOTS] = line
            stage_ref[d, SLOTS : SLOTS + PAD, SLOTS:] = jnp.zeros(
                (PAD, D - SLOTS), jnp.bfloat16
            )
            copy = pltpu.make_async_copy(stage_ref.at[d], out_ref.at[d], sems.at[d])
            copy.start()
            copies.append(copy)
    for copy in copies:
        copy.wait()


def messages(node_feats, send_rows, send_count, send_weight):
    return pl.pallas_call(
        message_kernel,
        in_specs=[WORDS, FAR, FAR, FAR],
        out_specs=FAR,
        out_shape=pltpu.HBM((8, SLOTS + PAD, D), jnp.bfloat16),
        scratch_shapes=[
            pltpu.VMEM((8, SLOTS), jnp.int32),
            pltpu.VMEM((8, SLOTS), jnp.bfloat16),
            pltpu.VMEM((NODES, D), jnp.bfloat16),
            pltpu.VMEM((8, SLOTS + PAD, D), jnp.bfloat16),
            pltpu.SemaphoreType.DMA((3,)),
            pltpu.SemaphoreType.DMA((8,)),
        ],
        compiler_params=params(12),
        cost_estimate=cost(2 * NODES * NODES * D, 5 * MIB),
        name="messages",
    )(far(send_count.reshape(8)), far(send_rows), far(send_weight), far(node_feats))


FIRST_HALVES = len(FIRST)
LATER_HALVES = len(SECOND) + len(THIRD)


def place_kernel(
    blocks_ref, tiles_ref, early_ref, later_ref, sums_ref, stage_ref, tally_ref, sems
):
    col = lax.axis_index("col")
    tally_ref[...] = jnp.zeros_like(tally_ref)
    stage_ref[...] = jnp.zeros_like(stage_ref)
    early_ref[...] = jnp.zeros_like(early_ref)

    def place(p, ref, column):
        first = half_index(col, p) * 4
        for t in range(4):
            at = pl.multiple_of(blocks_ref[first + t] * TB, TB)
            tile = tiles_ref[first + t]
            ref[pl.ds(at, TB), column * TB : (column + 1) * TB] = tile
            tally_ref[pl.ds(at, TB), :] += tile.astype(jnp.float32)

    for p in range(LATER_HALVES):
        place(FIRST_HALVES + p, stage_ref, p)
    copies = [pltpu.make_async_copy(stage_ref, later_ref, sems.at[0])]
    copies[0].start()
    for p in range(FIRST_HALVES):
        place(p, early_ref, p)
    copies.append(pltpu.make_async_copy(tally_ref, sums_ref, sems.at[1]))
    copies[1].start()
    for copy in copies:
        copy.wait()


def placed_tiles(tile_blocks, tile_weights):
    return pl.pallas_call(
        place_kernel,
        in_specs=[WORDS, ROWS],
        out_specs=[ROWS, FAR, FAR],
        out_shape=[
            pltpu.VMEM((NODES, FIRST_HALVES * TB), jnp.bfloat16),
            pltpu.HBM((NODES, LATER_HALVES * TB), jnp.bfloat16),
            pltpu.HBM((NODES, TB), jnp.float32),
        ],
        scratch_shapes=[
            pltpu.VMEM((NODES, LATER_HALVES * TB), jnp.bfloat16),
            pltpu.VMEM((NODES, TB), jnp.float32),
            pltpu.SemaphoreType.DMA((2,)),
        ],
        compiler_params=params(8),
        cost_estimate=cost(0, 12 * MIB),
        name="placed_tiles",
    )(tile_blocks.reshape(128), near(tile_weights))


def bias_kernel(bias_ref, out_ref):
    out_ref[...] = jnp.broadcast_to(bias_ref[...], (8, D))


def bias_rows(out_bias):
    return pl.pallas_call(
        bias_kernel,
        in_specs=[ROWS],
        out_specs=ROWS,
        out_shape=pltpu.VMEM((8, D), jnp.float32),
        compiler_params=params(2),
        cost_estimate=cost(1000, 1000),
        name="bias_rows",
    )(near(out_bias.reshape(1, D)))


def choose_kernel(up_ref, down_ref, out_ref):
    core = lax.axis_index("col") % 2

    @pl.when(core == 0)
    def _():
        out_ref[...] = up_ref[...]

    @pl.when(core == 1)
    def _():
        out_ref[...] = down_ref[...]


def choose(up, down):
    return pl.pallas_call(
        choose_kernel,
        in_specs=[ROWS, ROWS],
        out_specs=ROWS,
        out_shape=pltpu.VMEM(up.shape, up.dtype),
        compiler_params=params(2),
        cost_estimate=cost(1000, 1000),
        name="choose",
    )(near(up), near(down))


def self_kernel(feats_ref, weight_ref, bias_ref, out_ref, stage_ref, sems):
    copies = []
    for step in range(4):
        rows = slice(step * 256, (step + 1) * 256)
        stage_ref[rows, :] = product(feats_ref[rows, :], weight_ref[...]) + bias_ref[0:1, :]
        copy = pltpu.make_async_copy(
            stage_ref.at[rows], out_ref.at[rows], sems.at[step]
        )
        copy.start()
        copies.append(copy)
    for copy in copies:
        copy.wait()


def self_part(node_feats, self_weight, bias):
    return pl.pallas_call(
        self_kernel,
        in_specs=[ROWS, ROWS, ROWS],
        out_specs=FAR,
        out_shape=pltpu.HBM((NODES, D), jnp.float32),
        scratch_shapes=[
            pltpu.VMEM((NODES, D), jnp.float32),
            pltpu.SemaphoreType.DMA((4,)),
        ],
        compiler_params=params(8),
        cost_estimate=cost(1000, 1000),
        name="self_part",
    )(near(node_feats), near(self_weight), near(bias))


def hub_products(placed, parts):
    width = sum(part.shape[0] for part in parts)

    def body(placed_ref, *refs):
        out_ref, stage_ref, sems = refs[-3:]
        copies = []
        for step in range(4):
            rows = slice(step * 256, (step + 1) * 256)
            hubs = jnp.concatenate([ref[...] for ref in refs[: len(parts)]], axis=0)
            stage_ref[rows, :] = product(placed_ref[rows, :width], hubs)
            copy = pltpu.make_async_copy(
                stage_ref.at[rows], out_ref.at[rows], sems.at[step]
            )
            copy.start()
            copies.append(copy)
        for copy in copies:
            copy.wait()

    return pl.pallas_call(
        body,
        in_specs=[ROWS] * (1 + len(parts)),
        out_specs=FAR,
        out_shape=pltpu.HBM((NODES, D), jnp.float32),
        scratch_shapes=[pltpu.VMEM((NODES, D), jnp.float32), pltpu.SemaphoreType.DMA((4,))],
        compiler_params=params(16),
        cost_estimate=cost(int(3 * NODES * width * D), 15 * MIB),
        name="hub_products",
    )(near(placed), *[near(part) for part in parts])


def tail_part(sums, arrive_node, arrived):
    def body(at_ref, got_ref, sums_hbm, out_ref, scale_ref, hot_ref, sums_ref, sem):
        load = pltpu.make_async_copy(sums_hbm, sums_ref, sem)
        load.start()
        for step in range(4):
            rows = slice(step * 256, (step + 1) * 256)
            node = lax.broadcasted_iota(jnp.int32, (256, SLOTS), 0) + step * 256
            weights = jnp.zeros((256, SLOTS), jnp.float32)
            for o in range(8):
                hit = at_ref[o : o + 1, :] == node
                hot_ref[rows, o * SLOTS : (o + 1) * SLOTS] = jnp.where(hit, 1.0, 0.0).astype(
                    jnp.bfloat16
                )
                line = got_ref[o, SLOTS : SLOTS + 1, 0:SLOTS].astype(jnp.float32)
                weights = weights + jnp.where(hit, line, 0.0)
            scale_ref[rows, :] = weights
        load.wait()
        weight_sum = jnp.sum(scale_ref[...] + sums_ref[...], axis=-1, keepdims=True)
        scale_ref[...] = jnp.broadcast_to(lax.rsqrt(1.0 + weight_sum), (NODES, TB))
        for step in range(4):
            lanes = slice(step * 256, (step + 1) * 256)
            got = jnp.concatenate([got_ref[o, 0:SLOTS, lanes] for o in range(8)], axis=0)
            out_ref[:, lanes] = product(hot_ref[...], got)

    return pl.pallas_call(
        body,
        in_specs=[ROWS] * 2 + [FAR],
        out_specs=[ROWS, ROWS],
        out_shape=[pltpu.VMEM((NODES, D), jnp.float32), pltpu.VMEM((NODES, TB), jnp.float32)],
        scratch_shapes=[
            pltpu.VMEM((NODES, 8 * SLOTS), jnp.bfloat16),
            pltpu.VMEM((NODES, TB), jnp.float32),
            pltpu.SemaphoreType.DMA,
        ],
        compiler_params=params(10),
        cost_estimate=cost(2 * NODES * NODES * D, 10 * MIB),
        name="tail_part",
    )(near(arrive_node), near(arrived), far(sums))


def middle_part(placed, parts, carry, tail):
    width = sum(part.shape[0] for part in parts)

    def body(placed_ref, carry_ref, tail_ref, *refs):
        for step in range(4):
            lanes = slice(step * 256, (step + 1) * 256)
            hubs = jnp.concatenate([ref[:, lanes] for ref in refs[: len(parts)]], axis=0)
            total = product(placed_ref[:, 0:width], hubs) + carry_ref[:, lanes]
            refs[-1][:, lanes] = total + tail_ref[:, lanes]

    return pl.pallas_call(
        body,
        in_specs=[ROWS] * (3 + len(parts)),
        out_specs=ROWS,
        out_shape=pltpu.VMEM((NODES, D), jnp.float32),
        compiler_params=params(8),
        cost_estimate=cost(2 * NODES * width * D, 10 * MIB),
        name="middle_part",
    )(near(placed), near(carry), near(tail), *[near(part) for part in parts])


def last_part(placed, parts, scale, carry, base, neigh_weight):
    tm = 256

    width = sum(part.shape[0] for part in parts)
    first = placed.shape[1] - width

    def body(scale_ref, carry_ref, base_ref, weight_ref, placed_ref, *refs):
        out_ref, stage_ref, sems = refs[len(parts) :]
        copies = []
        for step in range(NODES // tm):
            rows = slice(step * tm, (step + 1) * tm)
            hubs = jnp.concatenate([ref[...] for ref in refs[: len(parts)]], axis=0)
            combined = carry_ref[rows, :] + product(placed_ref[rows, first:], hubs)
            neighbour = (combined * scale_ref[rows, 0:1]).astype(jnp.bfloat16)
            preact = base_ref[rows, :] + product(neighbour, weight_ref[...])
            hidden = jnp.maximum(preact, 0.0)
            norm = lax.rsqrt(jnp.mean(hidden * hidden, axis=-1, keepdims=True) + 1e-06)
            stage_ref[rows, :] = (hidden * norm).astype(jnp.bfloat16)
            copy = pltpu.make_async_copy(
                stage_ref.at[rows], out_ref.at[rows], sems.at[step]
            )
            copy.start()
            copies.append(copy)
        for copy in copies:
            copy.wait()

    return pl.pallas_call(
        body,
        in_specs=[ROWS] * (5 + len(parts)),
        out_specs=FAR,
        out_shape=pltpu.HBM((NODES, D), jnp.bfloat16),
        scratch_shapes=[
            pltpu.VMEM((NODES, D), jnp.bfloat16),
            pltpu.SemaphoreType.DMA((NODES // tm,)),
        ],
        compiler_params=params(12),
        cost_estimate=cost(2 * NODES * D * (width + D), 16 * MIB),
        name="last_part",
    )(
        *[near(value) for value in (scale, carry, base, neigh_weight, placed, *parts)],
    )


def shards(
    node_feats,
    hub_feats,
    self_weight,
    neigh_weight,
    out_bias,
    tile_weights,
    tile_blocks,
    send_rows,
    send_count,
    send_weight,
    arrive_node,
):
    own = hub_feats
    across = send(own, ACROSS)
    up = send(own, UP)
    down = send(own, DOWN)

    message = messages(node_feats, send_rows, send_count, send_weight)

    out_bias, own_k, message = lax.optimization_barrier((out_bias, own, message))
    arrived = lax.all_to_all(message, "row", split_axis=0, concat_axis=0, tiled=True)
    own_c = send(own_k, CORE)
    bias = bias_rows(out_bias)
    up, down, across, own_c, bias = lax.optimization_barrier((up, down, across, own_c, bias))
    two = send(choose(up, down), ONWARD)
    across_c = send(across, CORE)
    up_c = send(up, CORE)
    down_c = send(down, CORE)
    placed, placed_later, sums = placed_tiles(tile_blocks, tile_weights)

    two, across, across_c, up_c, down_c, placed, bias = lax.optimization_barrier(
        (two, across, across_c, up_c, down_c, placed, bias)
    )
    up_x = send(across, UP)
    down_x = send(across, DOWN)
    two_x = send(two, ACROSS)
    two_c = send(two, CORE)
    carry = hub_products(
        placed, [own, across, up, down, own_c, across_c, up_c, down_c]
    )

    base = self_part(node_feats, self_weight, bias)
    two_x, base, carry = lax.optimization_barrier((two_x, base, carry))
    two_xc = send(two_x, CORE)
    tail, scale = tail_part(sums, arrive_node, arrived)

    up_x, down_x, two_x, two_xc, two_c, carry, tail = lax.optimization_barrier(
        (up_x, down_x, two_x, two_xc, two_c, carry, tail)
    )
    late = [send(up_x, CORE), send(down_x, CORE), two_xc]
    carry = middle_part(placed_later, [two, two_c, up_x, down_x, two_x], carry, tail)
    return last_part(placed_later, late, scale, carry, base, neigh_weight)


def solution(mesh):
    placed = (
        P(("row", "col"), None),
        P("col", None),
        P(),
        P(),
        P(),
        P(("row", "col"), None, None),
        P(("row", "col"), None),
        P("row", "col"),
        P("row", "col"),
        P("row", "col"),
        P("row", "col"),
    )
    return jax.shard_map(
        shards, mesh=mesh, in_specs=placed, out_specs=P(("row", "col"), None), check_vma=False
    )
```
